128 devices in a mesh: group: 8 (over y, core), ingroup: 16 (over z, x).
Axes of the slice: x: 4, y: 4, z: 4, core: 2. Of those that a mesh axis runs over, the one named last changes fastest.
Arguments:
- context: bfloat16 [2048, 8192], P('group', 'ingroup'), may hold values from -6 to 6
- out_proj: bfloat16 [8192, 7168], P('ingroup'), may hold values from -0.0625 to 0.0625
- residual: bfloat16 [2048, 7168], P(('group', 'ingroup')), may hold values from -6 to 6
- norm_gain: float32 [7168], replicated, may hold values from 0.25 to 1.75
- expert_ids: int32 [2048, 8], P(('group', 'ingroup')), may hold values from 0 to 31, as said below
- gates: bfloat16 [2048, 8], P(('group', 'ingroup')), may hold values from 0.099609375 to 1
- gate_proj: bfloat16 [128, 7168, 256], P(('group', 'ingroup')), may hold values from -0.0625 to 0.0625
- up_proj: bfloat16 [128, 7168, 256], P(('group', 'ingroup')), may hold values from -0.0625 to 0.0625
- down_proj: bfloat16 [128, 256, 7168], P(('group', 'ingroup')), may hold values from -0.1875 to 0.1875
Outputs:
- layer_out: bfloat16 [2048, 7168], P(('group', 'ingroup'))
The draws below stay inside these ranges and needn't reach their ends.
Inputs may be any that keep to these rules, and one draw needn't show every extreme that they name: `expert_ids`: each row names 8 different experts, all of them in at most 4 expert groups, expert e lying in group e // 4.
All inputs are finite; a program needn't handle non-finite values.
Results may differ from the reference program's by a relative error of at most 0.012.
Values may be sent and summed in bfloat16 or wider, within the bound.
No kernel may reach another device: no remote copies, remote signals or barrier semaphores. Data moves between devices by JAX's collectives and lax.ppermute only.
A program may use at most 128 MiB of HBM per device.

```python
import math
import jax
import jax.numpy as jnp
from jax import lax

D = 7168
HEADS = 64
HEAD_DIM = 128
EXP_HIDDEN = 1024
TOPK = 8
TOPG = 4
SLICES = 4
TOK_DEV = 16
TOKENS = 2048
EXPERTS = 32
HID_SLICE = 256
ECAP = 5
N_GROUP = 8
N_INGROUP = 16


def draw_expert_ids(key, part):
    key_bias, key_jitter = jax.random.split(jax.random.fold_in(key, 17))
    favour = jax.random.randint(key_bias, (EXPERTS,), 0, 4) * 300
    jitter = jax.random.randint(key_jitter, (TOKENS, EXPERTS), 0, 1000)
    expert_iota = jnp.arange(EXPERTS, dtype=jnp.int32)
    scores = (favour[None, :] + jitter) * EXPERTS + expert_iota[None, :]
    grouped = scores.reshape(TOKENS, N_GROUP, EXPERTS // N_GROUP)
    best_two = lax.top_k(grouped, 2)[0]
    group_scores = jnp.sum(best_two, axis=2) * N_GROUP + jnp.arange(N_GROUP, dtype=jnp.int32)[None, :]
    top_groups = lax.top_k(group_scores, TOPG)[1]
    allowed = jnp.any(top_groups[:, :, None] == jnp.arange(N_GROUP, dtype=jnp.int32)[None, None, :], axis=1)
    allowed_experts = jnp.repeat(allowed, EXPERTS // N_GROUP, axis=1)
    masked = jnp.where(allowed_experts, scores, -1)
    return lax.top_k(masked, TOPK)[1].astype(jnp.int32)


def block_scale(key, extent, cuts, smallest, top_value):
    loudness = 1.0
    for dim, shards_of in cuts:
        steps = jax.random.uniform(jax.random.fold_in(jax.random.fold_in(key, 6), dim), (shards_of,), jnp.float32, smallest / len(cuts), top_value / len(cuts))
        loudness = loudness * jnp.repeat(jnp.exp(steps), extent[dim] // shards_of).reshape((-1,) + (1,) * (len(extent) - 1 - dim))
    return loudness


def bell_draw(own_key, dims, spread, reach, shards=(), kind=jnp.bfloat16):
    entries = spread * jax.random.normal(own_key, dims, jnp.float32)
    if shards:
        entries = entries * block_scale(own_key, dims, shards, -0.22, 0.18)
    return jnp.clip(entries, -reach, reach).astype(kind)


def setup_inputs(seed: int = 0) -> dict:
    keys = jax.random.split(jax.random.key(seed), 10)
    context = bell_draw(keys[0], (TOKENS, HEADS * HEAD_DIM), 1.0, 6.0, ((0, 8), (1, 16)))
    out_proj = bell_draw(keys[1], (HEADS * HEAD_DIM, D), (HEADS * HEAD_DIM) ** -0.5, 0.0625, ((0, 16),))
    residual = bell_draw(keys[2], (TOKENS, D), 1.0, 6.0, ((0, 128),))
    norm_gain = jnp.clip(1.0 + 0.15 * jax.random.normal(keys[3], (D,), jnp.float32), 0.25, 1.75)
    expert_ids = draw_expert_ids(jax.random.fold_in(keys[9], 71), 0)
    gates = jnp.clip(jnp.exp(math.log(1.0) - 2.306499 * jax.random.uniform(keys[5], (TOKENS, TOPK), jnp.float32) ** block_scale(keys[5], (TOKENS, TOPK), ((0, 128),), -0.2, 0.2)), 0.099609375, 1.0).astype(jnp.bfloat16)
    gate_proj = bell_draw(keys[6], (EXPERTS * SLICES, D, HID_SLICE), D ** -0.5, 0.0625, ((0, 128),))
    up_proj = bell_draw(keys[7], (EXPERTS * SLICES, D, HID_SLICE), D ** -0.5, 0.0625, ((0, 128),))
    down_proj = bell_draw(keys[8], (EXPERTS * SLICES, HID_SLICE, D), EXP_HIDDEN ** -0.5, 0.1875, ((0, 128),))
    return {"context": context, "out_proj": out_proj, "residual": residual, "norm_gain": norm_gain, "expert_ids": expert_ids, "gates": gates, "gate_proj": gate_proj, "up_proj": up_proj, "down_proj": down_proj}


def reference(context, out_proj, residual, norm_gain, expert_ids, gates, gate_proj, up_proj, down_proj):
    attended = jnp.dot(context, out_proj, preferred_element_type=jnp.float32)
    hidden = (residual.astype(jnp.float32) + attended).astype(jnp.bfloat16)
    hidden_wide = hidden.astype(jnp.float32)
    inverse = lax.rsqrt(lax.optimization_barrier(jnp.mean(hidden_wide * hidden_wide, axis=1, keepdims=True)) + 1e-06)
    normed = (hidden_wide * inverse * norm_gain).astype(jnp.bfloat16)
    device_total = N_GROUP * N_INGROUP
    slot_total = device_total * ECAP
    expert_iota = jnp.arange(EXPERTS, dtype=jnp.int32)
    matches = expert_ids[:, :, None] == expert_iota[None, None, :]
    picked = jnp.any(matches, axis=1)
    weighted = lax.optimization_barrier(jnp.sum(jnp.where(matches, gates.astype(jnp.float32)[:, :, None], jnp.float32(0)), axis=1))
    picked_count = picked.astype(jnp.int32)
    by_device = picked_count.reshape(device_total, TOK_DEV, EXPERTS)
    ranking = (jnp.cumsum(by_device, axis=1) - by_device).reshape(TOKENS, EXPERTS)
    admitted = picked & (ranking < ECAP)
    token_iota = jnp.arange(TOKENS, dtype=jnp.int32)
    owner = token_iota // TOK_DEV
    position = jnp.where(admitted, owner[:, None] * ECAP + ranking, slot_total).astype(jnp.int32)
    expert_index = jnp.broadcast_to(expert_iota[None, :], (TOKENS, EXPERTS))
    token_index = jnp.broadcast_to(token_iota[:, None], (TOKENS, EXPERTS))
    slot_tokens = jnp.zeros((EXPERTS, slot_total), jnp.int32).at[expert_index, position].set(token_index, mode='drop')
    filled = jnp.zeros((EXPERTS, slot_total), jnp.float32).at[expert_index, position].set(weighted, mode='drop')

    def one_expert(mixture, expert):
        gathered = jnp.take(normed, slot_tokens[expert], axis=0)
        summed = jnp.zeros((slot_total, D), jnp.float32)
        for slice_index in range(SLICES):
            block_index = expert * SLICES + slice_index
            gate_part = jnp.dot(gathered, gate_proj[block_index], preferred_element_type=jnp.float32)
            up_part = jnp.dot(gathered, up_proj[block_index], preferred_element_type=jnp.float32)
            activated = (jax.nn.silu(gate_part) * up_part).astype(jnp.bfloat16)
            partial_out = jnp.dot(activated, down_proj[block_index], preferred_element_type=jnp.float32).astype(jnp.bfloat16)
            summed = summed + partial_out.astype(jnp.float32)
        mixture = mixture.at[slot_tokens[expert]].add(summed * filled[expert][:, None])
        return (mixture, jnp.int32(0))
    mixture, unused = lax.scan(one_expert, jnp.zeros((TOKENS, D), jnp.float32), expert_iota)
    return (hidden_wide + mixture).astype(jnp.bfloat16)
```

```python
import jax
import jax.numpy as jnp
from jax import lax
from jax.sharding import Mesh
from jax.sharding import PartitionSpec as P

TOPK = 8
SLICES = 4
F32 = jnp.float32
BF16 = jnp.bfloat16


def shift(value, axis, amount):
    size = lax.axis_size(axis)
    return lax.ppermute(value, axis, [(i, (i + amount) % size) for i in range(size)])


def exchange(value, axes):
    return lax.all_to_all(value, axes, split_axis=0, concat_axis=0, tiled=True)


def local(context, out_proj, residual, norm_gain, expert_ids, gates, gate_proj, up_proj, down_proj):
    ny, nc, nz, nx = (lax.axis_size(a) for a in ("y", "c", "z", "x"))
    rows_here, width = residual.shape
    quarter = width // nx
    experts_total = ny * nc * nz
    capacity = min(rows_here, max(2, rows_here * TOPK * 5 // (4 * experts_total)))
    x = lax.axis_index("x")
    c = lax.axis_index("c")

    def cut(k):
        at = lax.rem(x + k, nx) * quarter
        gate_up = jnp.concatenate(
            [
                lax.dynamic_slice(gate_proj[0], (at, 0), (quarter, gate_proj.shape[2])),
                lax.dynamic_slice(up_proj[0], (at, 0), (quarter, up_proj.shape[2])),
            ],
            axis=1,
        )
        down = lax.dynamic_slice(down_proj[0], (0, at), (down_proj.shape[1], quarter))
        return gate_up, down

    pieces = [cut(k) for k in range(nx)]
    gate_up_by = [p[0] if k == 0 else shift(p[0], "x", k) for k, p in enumerate(pieces)]
    down_by = [p[1] if k == 0 else shift(p[1], "x", k) for k, p in enumerate(pieces)]

    meta = jnp.concatenate([expert_ids.astype(BF16), gates], axis=1)
    meta = jnp.pad(meta, ((0, 0), (0, 128 - meta.shape[1])))
    res_out = residual.reshape(rows_here, nx, quarter).transpose(1, 0, 2)
    res_out = jnp.concatenate([res_out, jnp.broadcast_to(meta[None], (nx,) + meta.shape)], axis=2)
    res_in = exchange(res_out, "x").reshape(nx * rows_here, quarter + 128)
    res_quarter = res_in[:, :quarter]
    meta_own = res_in[:, quarter:]
    meta_all = jnp.concatenate([meta_own, shift(meta_own, "c", 1)], axis=0)
    tokens = nc * nx * rows_here
    ids = meta_all[:, :TOPK].astype(jnp.int32)
    gate_vals = meta_all[:, TOPK : 2 * TOPK].astype(F32)

    places = ny * nz
    place = jnp.arange(places, dtype=jnp.int32)
    expert_of = ((place // nz) * nc + c) * nz + lax.rem(place, nz)
    matches = ids[:, :, None] == expert_of[None, None, :]
    picked = jnp.any(matches, axis=1).astype(jnp.int32)
    weighted = jnp.sum(jnp.where(matches, gate_vals[:, :, None], F32(0)), axis=1)
    by_device = picked.reshape(nc * nx, rows_here, places)
    ranking = jnp.cumsum(by_device, axis=1) - by_device
    admitted = (by_device > 0) & (ranking < capacity)
    device_iota = jnp.arange(nc * nx, dtype=jnp.int32)[:, None, None]
    slot = jnp.where(admitted, device_iota * capacity + ranking, -1).reshape(tokens, places)
    slots = nc * nx * capacity
    slot_iota = jnp.arange(slots, dtype=jnp.int32)
    chosen = slot.T[:, None, :] == slot_iota[None, :, None]
    selector = chosen.astype(BF16).reshape(places * slots, tokens)
    scaled = jnp.where(chosen, weighted.T[:, None, :], F32(0)).astype(BF16)
    scaled = scaled.reshape(places * slots, tokens)

    part = jnp.dot(context, out_proj, preferred_element_type=F32).astype(BF16)
    part = exchange(part.reshape(nz, nx * rows_here, width), "z")
    part = jnp.sum(part.astype(F32), axis=0).astype(BF16)
    part = part.reshape(nx * rows_here, nx, quarter).transpose(1, 0, 2)
    part = exchange(part, "x")
    attended = jnp.sum(part.astype(F32), axis=0)
    hidden = (res_quarter.astype(F32) + attended).astype(BF16)
    hidden_wide = hidden.astype(F32)
    square = jnp.sum(hidden_wide * hidden_wide, axis=1, keepdims=True)
    square = square + shift(square, "x", 1) + shift(square, "x", 2) + shift(square, "x", 3)
    inverse = lax.rsqrt(square / width + 1e-06)
    gain = lax.dynamic_slice(norm_gain, (x * quarter,), (quarter,))
    normed = (hidden_wide * inverse * gain[None, :]).astype(BF16)

    normed_all = jnp.concatenate([normed, shift(normed, "c", 1)], axis=0)
    outgoing = jnp.dot(selector, normed_all, preferred_element_type=F32).astype(BF16)
    arrived = exchange(outgoing.reshape(places, slots, quarter), ("y", "z"))
    arrived = arrived.reshape(places * slots, quarter)

    total = None
    for k in (2, 1, 3, 0):
        piece = jnp.dot(arrived, gate_up_by[k], preferred_element_type=F32)
        if k:
            piece = shift(piece.astype(BF16), "x", -k).astype(F32)
        total = piece if total is None else total + piece
    hid = total.shape[1] // 2
    activated = (jax.nn.silu(total[:, :hid]) * total[:, hid:]).astype(BF16)
    result = None
    for k in range(nx):
        block = activated if k == 0 else shift(activated, "x", k)
        piece = jnp.dot(block, down_by[k], preferred_element_type=F32)
        result = piece if result is None else result + piece

    returned = exchange(result.astype(BF16).reshape(places, slots, quarter), ("y", "z"))
    returned = returned.reshape(places * slots, quarter)
    mixture = lax.dot_general(
        scaled, returned, (((0,), (0,)), ((), ())), preferred_element_type=F32
    )
    half = tokens // nc
    mixture = mixture[:half] + shift(mixture[half:], "c", 1)
    out = (hidden_wide + mixture).astype(BF16)
    out = exchange(out.reshape(nx, rows_here, quarter), "x")
    return out.transpose(1, 0, 2).reshape(rows_here, width)


def solution(mesh):
    y = 4
    grid = Mesh(mesh.devices.reshape(y, 2, 4, 4), ("y", "c", "z", "x"))
    group, member = ("y", "c"), ("z", "x")
    owner = group + member
    in_specs = (
        P(group, member),
        P(member, None),
        P(owner, None),
        P(),
        P(owner, None),
        P(owner, None),
        P(owner, None, None),
        P(owner, None, None),
        P(owner, None, None),
    )
    return jax.shard_map(
        local, mesh=grid, in_specs=in_specs, out_specs=P(owner, None), check_vma=False
    )
```

```python
import jax
import jax.numpy as jnp
from jax import lax
from jax.experimental import pallas as pl
from jax.experimental.pallas import tpu as pltpu
from jax.sharding import Mesh
from jax.sharding import PartitionSpec as P

TOPK = 8
F32 = jnp.float32
BF16 = jnp.bfloat16


def shift(value, axis, amount):
    size = lax.axis_size(axis)
    return lax.ppermute(value, axis, [(i, (i + amount) % size) for i in range(size)])


def exchange(value, axes):
    return lax.all_to_all(value, axes, split_axis=0, concat_axis=0, tiled=True)


def mate_of(c, x):
    return x ^ 1 if c == 0 else x ^ 3


def twin_of(c, x):
    return x ^ 3 if c == 0 else x ^ 1


def from_places(value, source):
    pairs = []
    for c in range(2):
        for x in range(4):
            sc, sx = source(c, x)
            pairs.append((sc * 4 + sx, c * 4 + x))
    return lax.ppermute(value, ("c", "x"), pairs)


def project_body(mine_ref, a_ref, b_ref, r_ref, o_ref, acc_ref):
    own = r_ref.shape[0]
    acc_ref[...] = jnp.dot(a_ref[...], b_ref[...], preferred_element_type=F32)
    here = pl.ds(pl.multiple_of(mine_ref[0] * own, own), own)
    acc_ref[here, :] += r_ref[...].astype(F32)
    o_ref[0] = acc_ref[...].astype(BF16)


def project(mine, context, weight, residual, blocks):
    rows, depth = context.shape
    own, width = residual.shape
    cut = width // blocks
    halves = 2
    step = cut // halves
    return pl.pallas_call(
        project_body,
        out_shape=jax.ShapeDtypeStruct((blocks, rows, cut), BF16),
        grid_spec=pltpu.PrefetchScalarGridSpec(
            num_scalar_prefetch=1,
            grid=(blocks, halves),
            in_specs=[
                pl.BlockSpec((rows, depth), lambda q, j, m: (0, 0)),
                pl.BlockSpec((depth, step), lambda q, j, m: (0, q * halves + j)),
                pl.BlockSpec((own, step), lambda q, j, m: (0, q * halves + j)),
            ],
            out_specs=pl.BlockSpec((1, rows, step), lambda q, j, m: (q, 0, j)),
            scratch_shapes=[pltpu.VMEM((rows, step), F32)],
        ),
        compiler_params=pltpu.CompilerParams(vmem_limit_bytes=56 << 20),
        cost_estimate=pl.CostEstimate(
            flops=2 * rows * depth * width,
            bytes_accessed=2 * (rows * depth + depth * width + rows * width),
            transcendentals=0,
        ),
    )(mine, context, weight, residual)


def first_body(a_ref, gain_ref, w_ref, g_ref, s_ref, o_ref, acc_ref, sq_ref):
    step = pl.program_id(0)

    @pl.when(step == 0)
    def _():
        acc_ref[...] = jnp.zeros_like(acc_ref)
        sq_ref[...] = jnp.zeros_like(sq_ref)

    wide = a_ref[...].astype(F32)
    squares = wide * wide
    lanes = sq_ref.shape[1]
    partial = squares[:, :lanes]
    for i in range(1, squares.shape[1] // lanes):
        partial += squares[:, i * lanes : (i + 1) * lanes]
    sq_ref[...] += partial
    gained = (wide * gain_ref[...]).astype(BF16)
    g_ref[...] = gained
    acc_ref[...] += jnp.dot(gained, w_ref[...], preferred_element_type=F32)

    @pl.when(step == pl.num_programs(0) - 1)
    def _():
        o_ref[...] = acc_ref[...].astype(BF16)
        s_ref[...] = jnp.sum(sq_ref[...], axis=1, keepdims=True)


def first_product(arrived, gain, weight):
    rows, depth = arrived.shape
    cols = weight.shape[1]
    step = 512
    return pl.pallas_call(
        first_body,
        out_shape=(
            jax.ShapeDtypeStruct((rows, depth), BF16),
            jax.ShapeDtypeStruct((rows, 1), F32),
            jax.ShapeDtypeStruct((rows, cols), BF16),
        ),
        grid=(depth // step,),
        in_specs=[
            pl.BlockSpec((rows, step), lambda k: (0, k)),
            pl.BlockSpec((1, step), lambda k: (0, k)),
            pl.BlockSpec((step, cols), lambda k: (k, 0)),
        ],
        out_specs=(
            pl.BlockSpec((rows, step), lambda k: (0, k)),
            pl.BlockSpec((rows, 1), lambda k: (0, 0)),
            pl.BlockSpec((rows, cols), lambda k: (0, 0)),
        ),
        scratch_shapes=[pltpu.VMEM((rows, cols), F32), pltpu.VMEM((rows, 128), F32)],
        compiler_params=pltpu.CompilerParams(vmem_limit_bytes=24 << 20),
        cost_estimate=pl.CostEstimate(
            flops=2 * rows * depth * cols,
            bytes_accessed=2 * (2 * rows * depth + depth * cols + rows * cols),
            transcendentals=0,
        ),
    )(arrived, gain[None, :], weight)


def pack_body(at_ref, g_ref, u_ref, o_ref):
    h = g_ref.shape[2]
    o_ref[:, :h] = g_ref[0]
    o_ref[:, h:] = u_ref[0]


def pack(at, gate, up):
    deep, h = gate.shape[1:]
    cut = deep // 4
    steps = at.shape[0]
    return pl.pallas_call(
        pack_body,
        out_shape=jax.ShapeDtypeStruct((steps * cut, 2 * h), BF16),
        grid_spec=pltpu.PrefetchScalarGridSpec(
            num_scalar_prefetch=1,
            grid=(steps,),
            in_specs=[
                pl.BlockSpec((1, cut, h), lambda i, at: (0, at[i], 0)),
                pl.BlockSpec((1, cut, h), lambda i, at: (0, at[i], 0)),
            ],
            out_specs=pl.BlockSpec((cut, 2 * h), lambda i, at: (i, 0)),
        ),
        compiler_params=pltpu.CompilerParams(vmem_limit_bytes=56 << 20),
        cost_estimate=pl.CostEstimate(
            flops=0, bytes_accessed=8 * steps * cut * h, transcendentals=0
        ),
    )(at, gate, up)


def local(context, out_proj, residual, norm_gain, expert_ids, gates, gate_proj, up_proj, down_proj):
    ny, nc, nz, nx = (lax.axis_size(a) for a in ("y", "c", "z", "x"))
    rows_here, width = residual.shape
    quarter = width // nx
    experts_total = ny * nc * nz
    capacity = min(rows_here, max(2, rows_here * TOPK * 5 // (4 * experts_total)))
    x = lax.axis_index("x")
    c = lax.axis_index("c")
    mate = jnp.where(c == 0, x ^ 1, x ^ 3)
    twin = jnp.where(c == 0, x ^ 3, x ^ 1)
    tokens_core = nx * rows_here
    tokens = nc * tokens_core

    mine = lax.axis_index("z") * nx + x
    part = project(mine[None].astype(jnp.int32), context, out_proj, residual, nx)

    meta = jnp.concatenate([expert_ids.astype(BF16), gates], axis=1)
    meta = jnp.pad(meta, ((0, 0), (0, 128 - meta.shape[1])))
    came = [meta] + [shift(meta, "x", k) for k in range(1, nx)]
    part, came = lax.optimization_barrier((part, came))
    part = exchange(part.reshape(nx * nz, tokens_core, quarter), ("x", "z"))
    ring = [came[(nx - m) % nx] for m in range(nx)]
    ring = jnp.concatenate(ring + ring[:-1], axis=0)
    meta_own = lax.dynamic_slice(
        ring, (lax.rem(nx - x, nx) * rows_here, jnp.int32(0)), (tokens_core, meta.shape[1])
    )
    meta_all = jnp.concatenate([meta_own, shift(meta_own, "c", 1)], axis=0)
    ids = meta_all[:, :TOPK].astype(jnp.int32)
    gate_vals = meta_all[:, TOPK : 2 * TOPK].astype(F32)

    places = ny * nz
    place = jnp.arange(places, dtype=jnp.int32)
    expert_of = ((place // nz) * nc + c) * nz + lax.rem(place, nz)
    matches = ids[:, :, None] == expert_of[None, None, :]
    picked = jnp.any(matches, axis=1).astype(jnp.int32)
    weighted = jnp.sum(jnp.where(matches, gate_vals[:, :, None], F32(0)), axis=1)
    by_device = picked.reshape(nc * nx, rows_here, places)
    ranking = jnp.cumsum(by_device, axis=1) - by_device
    admitted = (by_device > 0) & (ranking < capacity)
    device_iota = jnp.arange(nc * nx, dtype=jnp.int32)[:, None, None]
    slot = jnp.where(admitted, device_iota * capacity + ranking, -1).reshape(tokens, places)
    slots = nc * nx * capacity
    slot_iota = jnp.arange(slots, dtype=jnp.int32)
    chosen = slot.T[:, None, :] == slot_iota[None, :, None]
    selector = chosen.astype(BF16).reshape(places * slots, tokens)
    scaled = jnp.where(chosen, weighted.T[:, None, :], F32(0)).astype(BF16)
    scaled = scaled.reshape(places * slots, tokens)
    kept = pack(jnp.stack([x, twin]).astype(jnp.int32), gate_proj, up_proj)
    given = pack(jnp.stack([mate, x ^ 2]).astype(jnp.int32), gate_proj, up_proj)

    def cut_down(k):
        at = lax.rem(x + k, nx) * quarter
        return lax.dynamic_slice(down_proj[0], (0, at), (down_proj.shape[1], quarter))

    down_cut = [cut_down(k) for k in range(nx)]
    selector, scaled, part, kept, given, down_cut = lax.optimization_barrier(
        (selector, scaled, part, kept, given, down_cut)
    )

    hidden = jnp.sum(part.astype(F32), axis=0).astype(BF16)
    hidden_wide = hidden.astype(F32)

    twin_own = from_places(hidden, lambda c, x: (c, twin_of(c, x)))
    near_other = from_places(hidden, lambda c, x: (1 - c, x))
    twin_other = from_places(hidden, lambda c, x: (1 - c, twin_of(c, x)))
    rows = jnp.concatenate(
        [
            jnp.concatenate([hidden, near_other], axis=0),
            jnp.concatenate([twin_own, twin_other], axis=0),
        ],
        axis=1,
    )
    outgoing = jnp.dot(selector, rows, preferred_element_type=F32).astype(BF16)
    arrived = exchange(outgoing.reshape(places, slots, 2 * quarter), ("y", "z"))
    arrived = arrived.reshape(places * slots, 2 * quarter)

    taken = from_places(given, lambda c, x: (c, mate_of(c, x)))
    down_by = [down_cut[0]] + [shift(down_cut[k], "x", k) for k in range(1, nx)]
    arrived, taken, down_by = lax.optimization_barrier((arrived, taken, down_by))

    gain = jnp.concatenate(
        [lax.dynamic_slice(norm_gain, (q * quarter,), (quarter,)) for q in (x, twin)]
    )
    to_mate = lambda value: from_places(value, lambda c, x: (c, mate_of(c, x)))
    gained, square, theirs = first_product(arrived, gain, taken)
    came_back = to_mate(theirs)
    inverse = lax.rsqrt((square + to_mate(square)) / width + 1e-06)
    total = jnp.dot(gained, kept, preferred_element_type=F32) + came_back.astype(F32)
    total = total * inverse
    hid = total.shape[1] // 2
    activated = (jax.nn.silu(total[:, :hid]) * total[:, hid:]).astype(BF16)
    result = None
    for k in (0, 1, 3, 2):
        block = activated if k == 0 else shift(activated, "x", k)
        piece = jnp.dot(block, down_by[k], preferred_element_type=F32)
        result = piece if result is None else result + piece

    returned = exchange(result.astype(BF16).reshape(places, slots, quarter), ("y", "z"))
    returned = returned.reshape(places * slots, quarter)
    mixture = lax.dot_general(
        scaled, returned, (((0,), (0,)), ((), ())), preferred_element_type=F32
    )
    mixture = mixture[:tokens_core] + shift(mixture[tokens_core:], "c", 1)
    out = (hidden_wide + mixture).astype(BF16)
    out = exchange(out.reshape(nx, rows_here, quarter), "x")
    return out.transpose(1, 0, 2).reshape(rows_here, width)


def solution(mesh):
    grid = Mesh(mesh.devices.reshape(4, 2, 4, 4), ("y", "c", "z", "x"))
    group, member = ("y", "c"), ("z", "x")
    owner = group + member
    in_specs = (
        P(group, member),
        P(member, None),
        P(owner, None),
        P(),
        P(owner, None),
        P(owner, None),
        P(owner, None, None),
        P(owner, None, None),
        P(owner, None, None),
    )
    return jax.shard_map(
        local, mesh=grid, in_specs=in_specs, out_specs=P(owner, None), check_vma=False
    )
```

```python
import jax
import jax.numpy as jnp
from jax import lax
from jax.experimental import pallas as pl
from jax.experimental.pallas import tpu as pltpu
from jax.sharding import Mesh
from jax.sharding import PartitionSpec as P

TOPK = 8
F32 = jnp.float32
BF16 = jnp.bfloat16


def shift(value, axis, amount):
    size = lax.axis_size(axis)
    return lax.ppermute(value, axis, [(i, (i + amount) % size) for i in range(size)])


def exchange(value, axes):
    return lax.all_to_all(value, axes, split_axis=0, concat_axis=0, tiled=True)


def mate_of(c, x):
    return x ^ 1 if c == 0 else x ^ 3


def twin_of(c, x):
    return x ^ 3 if c == 0 else x ^ 1


def from_places(value, source):
    pairs = []
    for c in range(2):
        for x in range(4):
            sc, sx = source(c, x)
            pairs.append((sc * 4 + sx, c * 4 + x))
    return lax.ppermute(value, ("c", "x"), pairs)


def project_body(mine_ref, a_ref, b_ref, r_ref, o_ref, acc_ref):
    own = r_ref.shape[0]
    acc_ref[...] = jnp.dot(a_ref[...], b_ref[...], preferred_element_type=F32)
    here = pl.ds(pl.multiple_of(mine_ref[0] * own, own), own)
    acc_ref[here, :] += r_ref[...].astype(F32)
    o_ref[0] = acc_ref[...].astype(BF16)


def project(mine, context, weight, residual, blocks):
    rows, depth = context.shape
    own, width = residual.shape
    cut = width // blocks
    halves = 1
    step = cut // halves
    return pl.pallas_call(
        project_body,
        out_shape=jax.ShapeDtypeStruct((blocks, rows, cut), BF16),
        grid_spec=pltpu.PrefetchScalarGridSpec(
            num_scalar_prefetch=1,
            grid=(blocks, halves),
            in_specs=[
                pl.BlockSpec((rows, depth), lambda q, j, m: (0, 0)),
                pl.BlockSpec((depth, step), lambda q, j, m: (0, q * halves + j)),
                pl.BlockSpec((own, step), lambda q, j, m: (0, q * halves + j)),
            ],
            out_specs=pl.BlockSpec((1, rows, step), lambda q, j, m: (q, 0, j)),
            scratch_shapes=[pltpu.VMEM((rows, step), F32)],
        ),
        compiler_params=pltpu.CompilerParams(vmem_limit_bytes=56 << 20),
        cost_estimate=pl.CostEstimate(
            flops=2 * rows * depth * width,
            bytes_accessed=2 * (rows * depth + depth * width + rows * width),
            transcendentals=0,
        ),
    )(mine, context, weight, residual)


def first_body(a_ref, gain_ref, w_ref, g_ref, s_ref, o_ref):
    depth = a_ref.shape[1]
    step = depth // 7
    total = None
    squares = None
    for at in range(0, depth, step):
        wide = a_ref[:, at : at + step].astype(F32)
        for i in range(0, step, 128):
            part = wide[:, i : i + 128]
            squares = part * part if squares is None else squares + part * part
        gained = (wide * gain_ref[:, at : at + step]).astype(BF16)
        g_ref[:, at : at + step] = gained
        piece = jnp.dot(gained, w_ref[at : at + step, :], preferred_element_type=F32)
        total = piece if total is None else total + piece
    o_ref[...] = total.astype(BF16)
    s_ref[...] = jnp.sum(squares, axis=1, keepdims=True)


def first_product(arrived, gain, weight):
    rows, depth = arrived.shape
    cols = weight.shape[1]
    whole = pl.BlockSpec(memory_space=pltpu.VMEM)
    return pl.pallas_call(
        first_body,
        out_shape=(
            jax.ShapeDtypeStruct((rows, depth), BF16),
            jax.ShapeDtypeStruct((rows, 1), F32),
            jax.ShapeDtypeStruct((rows, cols), BF16),
        ),
        in_specs=[whole] * 3,
        out_specs=(whole,) * 3,
        compiler_params=pltpu.CompilerParams(vmem_limit_bytes=32 << 20),
        cost_estimate=pl.CostEstimate(
            flops=2 * rows * depth * cols,
            bytes_accessed=2 * (2 * rows * depth + depth * cols + rows * cols),
            transcendentals=0,
        ),
    )(arrived, gain[None, :], weight)


def pack_body(at_ref, g_ref, u_ref, o_ref):
    h = g_ref.shape[2]
    o_ref[:, :h] = g_ref[0]
    o_ref[:, h:] = u_ref[0]


def pack(at, gate, up):
    deep, h = gate.shape[1:]
    cut = deep // 4
    steps = at.shape[0]
    return pl.pallas_call(
        pack_body,
        out_shape=jax.ShapeDtypeStruct((steps * cut, 2 * h), BF16),
        grid_spec=pltpu.PrefetchScalarGridSpec(
            num_scalar_prefetch=1,
            grid=(steps,),
            in_specs=[
                pl.BlockSpec((1, cut, h), lambda i, at: (0, at[i], 0)),
                pl.BlockSpec((1, cut, h), lambda i, at: (0, at[i], 0)),
            ],
            out_specs=pl.BlockSpec((cut, 2 * h), lambda i, at: (i, 0)),
        ),
        compiler_params=pltpu.CompilerParams(vmem_limit_bytes=56 << 20),
        cost_estimate=pl.CostEstimate(
            flops=0, bytes_accessed=8 * steps * cut * h, transcendentals=0
        ),
    )(at, gate, up)


def local(context, out_proj, residual, norm_gain, expert_ids, gates, gate_proj, up_proj, down_proj):
    ny, nc, nz, nx = (lax.axis_size(a) for a in ("y", "c", "z", "x"))
    rows_here, width = residual.shape
    quarter = width // nx
    experts_total = ny * nc * nz
    capacity = min(rows_here, max(2, rows_here * TOPK * 5 // (4 * experts_total)))
    x = lax.axis_index("x")
    c = lax.axis_index("c")
    mate = jnp.where(c == 0, x ^ 1, x ^ 3)
    twin = jnp.where(c == 0, x ^ 3, x ^ 1)
    tokens_core = nx * rows_here
    tokens = nc * tokens_core

    mine = lax.axis_index("z") * nx + x
    part = project(mine[None].astype(jnp.int32), context, out_proj, residual, nx)

    meta = jnp.concatenate([expert_ids.astype(BF16), gates], axis=1)
    meta = jnp.pad(meta, ((0, 0), (0, 128 - meta.shape[1])))
    came = [meta] + [shift(meta, "x", k) for k in range(1, nx)]
    part, came = lax.optimization_barrier((part, came))
    part = exchange(part.reshape(nx * nz, tokens_core, quarter), ("x", "z"))
    ring = [came[(nx - m) % nx] for m in range(nx)]
    ring = jnp.concatenate(ring + ring[:-1], axis=0)
    meta_own = lax.dynamic_slice(
        ring, (lax.rem(nx - x, nx) * rows_here, jnp.int32(0)), (tokens_core, meta.shape[1])
    )
    meta_all = jnp.concatenate([meta_own, shift(meta_own, "c", 1)], axis=0)
    ids = meta_all[:, :TOPK].astype(jnp.int32)
    gate_vals = meta_all[:, TOPK : 2 * TOPK].astype(F32)

    places = ny * nz
    place = jnp.arange(places, dtype=jnp.int32)
    expert_of = ((place // nz) * nc + c) * nz + lax.rem(place, nz)
    matches = ids[:, :, None] == expert_of[None, None, :]
    picked = jnp.any(matches, axis=1).astype(jnp.int32)
    weighted = jnp.sum(jnp.where(matches, gate_vals[:, :, None], F32(0)), axis=1)
    by_device = picked.reshape(nc * nx, rows_here, places)
    ranking = jnp.cumsum(by_device, axis=1) - by_device
    admitted = (by_device > 0) & (ranking < capacity)
    device_iota = jnp.arange(nc * nx, dtype=jnp.int32)[:, None, None]
    slot = jnp.where(admitted, device_iota * capacity + ranking, -1).reshape(tokens, places)
    slots = nc * nx * capacity
    slot_iota = jnp.arange(slots, dtype=jnp.int32)
    chosen = slot.T[:, None, :] == slot_iota[None, :, None]
    selector = chosen.astype(BF16).reshape(places * slots, tokens)
    scaled = jnp.where(chosen, weighted.T[:, None, :], F32(0)).astype(BF16)
    scaled = scaled.reshape(places * slots, tokens)
    kept = pack(jnp.stack([x, twin]).astype(jnp.int32), gate_proj, up_proj)
    given = pack(jnp.stack([mate, x ^ 2]).astype(jnp.int32), gate_proj, up_proj)

    def cut_down(k):
        at = lax.rem(x + k, nx) * quarter
        return lax.dynamic_slice(down_proj[0], (0, at), (down_proj.shape[1], quarter))

    down_cut = [cut_down(k) for k in range(nx)]
    selector, scaled, part, kept, given, down_cut = lax.optimization_barrier(
        (selector, scaled, part, kept, given, down_cut)
    )

    hidden = jnp.sum(part.astype(F32), axis=0).astype(BF16)
    hidden_wide = hidden.astype(F32)

    twin_own = from_places(hidden, lambda c, x: (c, twin_of(c, x)))
    near_other = from_places(hidden, lambda c, x: (1 - c, x))
    twin_other = from_places(hidden, lambda c, x: (1 - c, twin_of(c, x)))
    rows = jnp.concatenate(
        [
            jnp.concatenate([hidden, near_other], axis=0),
            jnp.concatenate([twin_own, twin_other], axis=0),
        ],
        axis=1,
    )
    outgoing = jnp.dot(selector, rows, preferred_element_type=F32).astype(BF16)
    arrived = exchange(outgoing.reshape(places, slots, 2 * quarter), ("y", "z"))
    arrived = arrived.reshape(places * slots, 2 * quarter)

    taken = from_places(given, lambda c, x: (c, mate_of(c, x)))
    half = down_cut[2].shape[0] // 2
    hop_up, hop_down = shift(down_cut[2][:half], "x", 1), shift(down_cut[2][half:], "x", -1)
    down_by = [down_cut[0], shift(down_cut[1], "x", 1), None, shift(down_cut[3], "x", 3)]
    arrived, taken, down_by[1], down_by[3], hop_up, hop_down = lax.optimization_barrier(
        (arrived, taken, down_by[1], down_by[3], hop_up, hop_down)
    )
    hop_up, hop_down = shift(hop_up, "x", 1), shift(hop_down, "x", -1)

    gain = jnp.concatenate(
        [lax.dynamic_slice(norm_gain, (q * quarter,), (quarter,)) for q in (x, twin)]
    )
    to_mate = lambda value: from_places(value, lambda c, x: (c, mate_of(c, x)))
    gained, square, theirs = first_product(arrived, gain, taken)
    theirs, hop_up, hop_down = lax.optimization_barrier((theirs, hop_up, hop_down))
    came_back = to_mate(theirs)
    inverse = lax.rsqrt((square + to_mate(square)) / width + 1e-06)
    total = jnp.dot(gained, kept, preferred_element_type=F32)
    total, came_back = lax.optimization_barrier((total, came_back))
    total = total + came_back.astype(F32)
    total = total * inverse
    hid = total.shape[1] // 2
    activated = (jax.nn.silu(total[:, :hid]) * total[:, hid:]).astype(BF16)
    result = jnp.dot(activated, down_by[0], preferred_element_type=F32)
    for k in (1, 3):
        block = shift(activated, "x", k)
        result += jnp.dot(block, down_by[k], preferred_element_type=F32)
    block = shift(activated, "x", 2)
    result += jnp.dot(block[:, :half], hop_up, preferred_element_type=F32)
    result += jnp.dot(block[:, half:], hop_down, preferred_element_type=F32)

    returned = exchange(result.astype(BF16).reshape(places, slots, quarter), ("y", "z"))
    returned = returned.reshape(places * slots, quarter)
    mixture = lax.dot_general(
        scaled, returned, (((0,), (0,)), ((), ())), preferred_element_type=F32
    )
    mixture = mixture[:tokens_core] + shift(mixture[tokens_core:], "c", 1)
    out = (hidden_wide + mixture).astype(BF16)
    out = exchange(out.reshape(nx, rows_here, quarter), "x")
    return out.transpose(1, 0, 2).reshape(rows_here, width)


def solution(mesh):
    grid = Mesh(mesh.devices.reshape(4, 2, 4, 4), ("y", "c", "z", "x"))
    group, member = ("y", "c"), ("z", "x")
    owner = group + member
    in_specs = (
        P(group, member),
        P(member, None),
        P(owner, None),
        P(),
        P(owner, None),
        P(owner, None),
        P(owner, None, None),
        P(owner, None, None),
        P(owner, None, None),
    )
    return jax.shard_map(
        local, mesh=grid, in_specs=in_specs, out_specs=P(owner, None), check_vma=False
    )
```

```python
import functools

import jax
import jax.numpy as jnp
from jax import lax
from jax.experimental import pallas as pl
from jax.experimental.pallas import tpu as pltpu
from jax.sharding import Mesh
from jax.sharding import PartitionSpec as P

TOPK = 8
F32 = jnp.float32
BF16 = jnp.bfloat16


def shift(value, axis, amount):
    size = lax.axis_size(axis)
    return lax.ppermute(value, axis, [(i, (i + amount) % size) for i in range(size)])


def exchange(value, axes):
    return lax.all_to_all(value, axes, split_axis=0, concat_axis=0, tiled=True)


def mate_of(c, x):
    return x ^ 1 if c == 0 else x ^ 3


def twin_of(c, x):
    return x ^ 3 if c == 0 else x ^ 1


def from_places(value, source):
    pairs = []
    for c in range(2):
        for x in range(4):
            sc, sx = source(c, x)
            pairs.append((sc * 4 + sx, c * 4 + x))
    return lax.ppermute(value, ("c", "x"), pairs)


def project_body(mine_ref, a_ref, b_ref, r_ref, o_ref, acc_ref):
    own = r_ref.shape[0]
    acc_ref[...] = jnp.dot(a_ref[...], b_ref[...], preferred_element_type=F32)
    here = pl.ds(pl.multiple_of(mine_ref[0] * own, own), own)
    acc_ref[here, :] += r_ref[...].astype(F32)
    o_ref[0] = acc_ref[...].astype(BF16)


def project(mine, context, weight, residual, blocks):
    rows, depth = context.shape
    own, width = residual.shape
    cut = width // blocks
    halves = 1
    step = cut // halves
    return pl.pallas_call(
        project_body,
        out_shape=jax.ShapeDtypeStruct((blocks, rows, cut), BF16),
        grid_spec=pltpu.PrefetchScalarGridSpec(
            num_scalar_prefetch=1,
            grid=(blocks, halves),
            in_specs=[
                pl.BlockSpec((rows, depth), lambda q, j, m: (0, 0)),
                pl.BlockSpec((depth, step), lambda q, j, m: (0, q * halves + j)),
                pl.BlockSpec((own, step), lambda q, j, m: (0, q * halves + j)),
            ],
            out_specs=pl.BlockSpec((1, rows, step), lambda q, j, m: (q, 0, j)),
            scratch_shapes=[pltpu.VMEM((rows, step), F32)],
        ),
        compiler_params=pltpu.CompilerParams(vmem_limit_bytes=56 << 20),
        cost_estimate=pl.CostEstimate(
            flops=2 * rows * depth * width,
            bytes_accessed=2 * (rows * depth + depth * width + rows * width),
            transcendentals=0,
        ),
    )(mine, context, weight, residual)


def first_body(a_ref, gain_ref, w_ref, g_ref, s_ref, o_ref):
    depth = a_ref.shape[1]
    h = w_ref.shape[1]
    squares = None
    for at in range(0, depth, 256):
        wide = a_ref[:, at : at + 256].astype(F32)
        for i in range(0, 256, 128):
            part = wide[:, i : i + 128]
            squares = part * part if squares is None else squares + part * part
        g_ref[:, at : at + 256] = (wide * gain_ref[:, at : at + 256]).astype(BF16)
    gained = g_ref[...]
    for i in range(2):
        o_ref[:, i * h : (i + 1) * h] = jnp.dot(
            gained, w_ref[i * depth : (i + 1) * depth, :], preferred_element_type=F32
        ).astype(BF16)
    s_ref[...] = jnp.sum(squares, axis=1, keepdims=True)


WHOLE = pl.BlockSpec(memory_space=pltpu.VMEM)


def first_product(arrived, gain, weight):
    rows, depth = arrived.shape
    cols = 2 * weight.shape[1]
    return pl.pallas_call(
        first_body,
        out_shape=(
            jax.ShapeDtypeStruct((rows, depth), BF16),
            jax.ShapeDtypeStruct((rows, 1), F32),
            jax.ShapeDtypeStruct((rows, cols), BF16),
        ),
        in_specs=[WHOLE] * 3,
        out_specs=(WHOLE,) * 3,
        compiler_params=pltpu.CompilerParams(vmem_limit_bytes=32 << 20),
        cost_estimate=pl.CostEstimate(
            flops=2 * rows * depth * cols,
            bytes_accessed=2 * (2 * rows * depth + depth * cols + rows * cols),
            transcendentals=0,
        ),
    )(arrived, gain, weight)


def down_body(start, *refs):
    own, from_mate, from_twin, from_far, w_own, w_mate, w_twin, w_far, o_ref = refs
    h = own.shape[1]
    for j in range(o_ref.shape[1] // h):
        cols = slice(j * h, (j + 1) * h)
        at = slice(start + j * h, start + (j + 1) * h)
        total = jnp.dot(own[...], w_own[:, cols], preferred_element_type=F32)
        total += jnp.dot(from_mate[...], w_mate[at, :], preferred_element_type=F32)
        total += jnp.dot(from_twin[...], w_twin[:, cols], preferred_element_type=F32)
        total += jnp.dot(from_far[...], w_far[cols, :], preferred_element_type=F32)
        o_ref[:, cols] = total.astype(BF16)


def down_product(blocks, weights, start):
    rows, h = blocks[0].shape
    cols = weights[0].shape[1]
    return pl.pallas_call(
        functools.partial(down_body, start),
        out_shape=jax.ShapeDtypeStruct((rows, cols), BF16),
        in_specs=[WHOLE] * 8,
        out_specs=WHOLE,
        compiler_params=pltpu.CompilerParams(vmem_limit_bytes=32 << 20),
        cost_estimate=pl.CostEstimate(
            flops=8 * rows * h * cols,
            bytes_accessed=2 * (4 * rows * h + 4 * h * cols + rows * cols),
            transcendentals=0,
        ),
    )(*blocks, *weights)


def bundle_body(at_ref, g_ref, u_ref, d_ref, o_ref):
    step = pl.program_id(0)
    h = o_ref.shape[1]

    @pl.when(step < 2)
    def _():
        o_ref[...] = g_ref[0]

    @pl.when((step >= 2) & (step < 4))
    def _():
        o_ref[...] = u_ref[0]

    @pl.when(step >= 4)
    def _():
        for j in range(d_ref.shape[2] // h):
            o_ref[j * h : (j + 1) * h, :] = d_ref[0, :, j * h : (j + 1) * h]


def bundle(at, gate, up, down):
    deep, h = gate.shape[1:]
    cut = deep // 4

    def pick(last_first):
        return lambda i, at: at[jnp.where(i <= last_first, 0, 1)]

    gate_at, up_at, down_at = pick(0), pick(2), pick(4)
    return pl.pallas_call(
        bundle_body,
        out_shape=jax.ShapeDtypeStruct((6 * cut, h), BF16),
        grid_spec=pltpu.PrefetchScalarGridSpec(
            num_scalar_prefetch=1,
            grid=(6,),
            in_specs=[
                pl.BlockSpec((1, cut, h), lambda i, at: (0, gate_at(i, at), 0)),
                pl.BlockSpec((1, cut, h), lambda i, at: (0, up_at(i, at), 0)),
                pl.BlockSpec((1, h, cut), lambda i, at: (0, 0, down_at(i, at))),
            ],
            out_specs=pl.BlockSpec((cut, h), lambda i, at: (i, 0)),
        ),
        compiler_params=pltpu.CompilerParams(vmem_limit_bytes=56 << 20),
        cost_estimate=pl.CostEstimate(
            flops=0, bytes_accessed=24 * cut * h, transcendentals=0
        ),
    )(at, gate, up, down)


def pack_body(at_ref, g_ref, u_ref, o_ref):
    h = g_ref.shape[2]
    o_ref[:, :h] = g_ref[0]
    o_ref[:, h:] = u_ref[0]


def pack(at, gate, up):
    deep, h = gate.shape[1:]
    cut = deep // 4
    steps = at.shape[0]
    return pl.pallas_call(
        pack_body,
        out_shape=jax.ShapeDtypeStruct((steps * cut, 2 * h), BF16),
        grid_spec=pltpu.PrefetchScalarGridSpec(
            num_scalar_prefetch=1,
            grid=(steps,),
            in_specs=[
                pl.BlockSpec((1, cut, h), lambda i, at: (0, at[i], 0)),
                pl.BlockSpec((1, cut, h), lambda i, at: (0, at[i], 0)),
            ],
            out_specs=pl.BlockSpec((cut, 2 * h), lambda i, at: (i, 0)),
        ),
        compiler_params=pltpu.CompilerParams(vmem_limit_bytes=56 << 20),
        cost_estimate=pl.CostEstimate(
            flops=0, bytes_accessed=8 * steps * cut * h, transcendentals=0
        ),
    )(at, gate, up)


def local(context, out_proj, residual, norm_gain, expert_ids, gates, gate_proj, up_proj, down_proj):
    ny, nc, nz, nx = (lax.axis_size(a) for a in ("y", "c", "z", "x"))
    rows_here, width = residual.shape
    quarter = width // nx
    experts_total = ny * nc * nz
    capacity = min(rows_here, max(2, rows_here * TOPK * 5 // (4 * experts_total)))
    x = lax.axis_index("x")
    c = lax.axis_index("c")
    mate = jnp.where(c == 0, x ^ 1, x ^ 3)
    twin = jnp.where(c == 0, x ^ 3, x ^ 1)
    tokens_core = nx * rows_here
    tokens = nc * tokens_core

    to_mate = lambda value: from_places(value, lambda c, x: (c, mate_of(c, x)))
    to_twin = lambda value: from_places(value, lambda c, x: (c, twin_of(c, x)))

    def cut_down(at):
        return lax.dynamic_slice(
            down_proj[0], (0, at * quarter), (down_proj.shape[1], quarter)
        )

    twin_cut, context = lax.optimization_barrier((cut_down(twin), context))
    twin_down = to_twin(twin_cut)

    mine = lax.axis_index("z") * nx + x
    part = project(mine[None].astype(jnp.int32), context, out_proj, residual, nx)

    meta = jnp.concatenate([expert_ids.astype(BF16), gates], axis=1)
    meta = jnp.pad(meta, ((0, 0), (0, 128 - meta.shape[1])))
    came = [meta] + [shift(meta, "x", k) for k in range(1, nx)]
    part, came, twin_down, down_proj = lax.optimization_barrier((part, came, twin_down, down_proj))
    part = exchange(part.reshape(nx * nz, tokens_core, quarter), ("x", "z"))
    ring = [came[(nx - m) % nx] for m in range(nx)]
    ring = jnp.concatenate(ring + ring[:-1], axis=0)
    meta_own = lax.dynamic_slice(
        ring, (lax.rem(nx - x, nx) * rows_here, jnp.int32(0)), (tokens_core, meta.shape[1])
    )
    meta_all = jnp.concatenate([meta_own, shift(meta_own, "c", 1)], axis=0)
    ids = meta_all[:, :TOPK].astype(jnp.int32)
    gate_vals = meta_all[:, TOPK : 2 * TOPK].astype(F32)

    places = ny * nz
    place = jnp.arange(places, dtype=jnp.int32)
    expert_of = ((place // nz) * nc + c) * nz + lax.rem(place, nz)
    matches = ids[:, :, None] == expert_of[None, None, :]
    picked = jnp.any(matches, axis=1).astype(jnp.int32)
    weighted = jnp.sum(jnp.where(matches, gate_vals[:, :, None], F32(0)), axis=1)
    by_device = picked.reshape(nc * nx, rows_here, places)
    ranking = jnp.cumsum(by_device, axis=1) - by_device
    admitted = (by_device > 0) & (ranking < capacity)
    device_iota = jnp.arange(nc * nx, dtype=jnp.int32)[:, None, None]
    slot = jnp.where(admitted, device_iota * capacity + ranking, -1).reshape(tokens, places)
    slots = nc * nx * capacity
    slot_iota = jnp.arange(slots, dtype=jnp.int32)
    chosen = slot.T[:, None, :] == slot_iota[None, :, None]
    selector = chosen.astype(BF16).reshape(places * slots, tokens)
    scaled = jnp.where(chosen, weighted.T[:, None, :], F32(0)).astype(BF16)
    scaled = scaled.reshape(places * slots, tokens)
    kept = pack(jnp.stack([x, twin]).astype(jnp.int32), gate_proj, up_proj)
    given = bundle(jnp.stack([mate, x ^ 2]).astype(jnp.int32), gate_proj, up_proj, down_proj)
    own_down = cut_down(x)
    gain = jnp.concatenate(
        [lax.dynamic_slice(norm_gain, (q * quarter,), (quarter,)) for q in (x, twin)]
    )[None, :]
    selector, scaled, part, kept, given, own_down, gain = lax.optimization_barrier(
        (selector, scaled, part, kept, given, own_down, gain)
    )

    hidden = jnp.sum(part.astype(F32), axis=0).astype(BF16)
    hidden_wide = hidden.astype(F32)

    twin_own = from_places(hidden, lambda c, x: (c, twin_of(c, x)))
    near_other = from_places(hidden, lambda c, x: (1 - c, x))
    twin_other = from_places(hidden, lambda c, x: (1 - c, twin_of(c, x)))
    twin_own, near_other, twin_other, given = lax.optimization_barrier(
        (twin_own, near_other, twin_other, given)
    )
    rows = jnp.concatenate(
        [
            jnp.concatenate([hidden, near_other], axis=0),
            jnp.concatenate([twin_own, twin_other], axis=0),
        ],
        axis=1,
    )
    outgoing = jnp.dot(selector, rows, preferred_element_type=F32).astype(BF16)
    arrived = exchange(outgoing.reshape(places, slots, 2 * quarter), ("y", "z"))
    arrived = arrived.reshape(places * slots, 2 * quarter)

    taken = to_mate(given)
    arrived, taken = lax.optimization_barrier((arrived, taken))
    gained, square, theirs = first_product(arrived, gain, taken)
    theirs, taken = lax.optimization_barrier((theirs, taken))
    deep = taken.shape[0] // 6
    far_down = to_twin(taken[5 * deep :])
    came_back = to_mate(theirs)
    inverse = lax.rsqrt((square + to_mate(square)) / width + 1e-06)
    total = jnp.dot(gained, kept, preferred_element_type=F32)
    total, came_back = lax.optimization_barrier((total, came_back))
    total = total + came_back.astype(F32)
    total = total * inverse
    hid = total.shape[1] // 2
    activated = (jax.nn.silu(total[:, :hid]) * total[:, hid:]).astype(BF16)
    activated, far_down = lax.optimization_barrier((activated, far_down))
    blocks = (activated, to_mate(activated), to_twin(activated), shift(activated, "x", 2))
    result = down_product(blocks, (own_down, taken, twin_down, far_down), 4 * deep)

    returned = exchange(result.reshape(places, slots, quarter), ("y", "z"))
    returned = returned.reshape(places * slots, quarter)
    mixture = lax.dot_general(
        scaled, returned, (((0,), (0,)), ((), ())), preferred_element_type=F32
    )
    mixture = mixture[:tokens_core] + shift(mixture[tokens_core:], "c", 1)
    out = (hidden_wide + mixture).astype(BF16)
    out = exchange(out.reshape(nx, rows_here, quarter), "x")
    return out.transpose(1, 0, 2).reshape(rows_here, width)


def solution(mesh):
    grid = Mesh(mesh.devices.reshape(4, 2, 4, 4), ("y", "c", "z", "x"))
    group, member = ("y", "c"), ("z", "x")
    owner = group + member
    in_specs = (
        P(group, member),
        P(member, None),
        P(owner, None),
        P(),
        P(owner, None),
        P(owner, None),
        P(owner, None, None),
        P(owner, None, None),
        P(owner, None, None),
    )
    return jax.shard_map(
        local, mesh=grid, in_specs=in_specs, out_specs=P(owner, None), check_vma=False
    )
```

```python
import functools

import jax
import jax.numpy as jnp
from jax import lax
from jax.experimental import pallas as pl
from jax.experimental.pallas import tpu as pltpu
from jax.sharding import Mesh
from jax.sharding import PartitionSpec as P

TOPK = 8
EARLY = 3
F32 = jnp.float32
BF16 = jnp.bfloat16


def shift(value, axis, amount):
    size = lax.axis_size(axis)
    return lax.ppermute(value, axis, [(i, (i + amount) % size) for i in range(size)])


def exchange(value, axes):
    return lax.all_to_all(value, axes, split_axis=0, concat_axis=0, tiled=True)


def mate_of(c, x):
    return x ^ 1 if c == 0 else x ^ 3


def twin_of(c, x):
    return x ^ 3 if c == 0 else x ^ 1


def from_places(value, source):
    pairs = []
    for c in range(2):
        for x in range(4):
            sc, sx = source(c, x)
            pairs.append((sc * 4 + sx, c * 4 + x))
    return lax.ppermute(value, ("c", "x"), pairs)


def project_body(mine_ref, a_ref, b_ref, r_ref, o_ref, acc_ref):
    own = r_ref.shape[0]
    acc_ref[...] = jnp.dot(a_ref[...], b_ref[...], preferred_element_type=F32)
    here = pl.ds(pl.multiple_of(mine_ref[0] * own, own), own)
    acc_ref[here, :] += r_ref[...].astype(F32)
    o_ref[0] = acc_ref[...].astype(BF16)


def project(mine, context, weight, residual, blocks):
    rows, depth = context.shape
    own, width = residual.shape
    cut = width // blocks
    halves = 1
    step = cut // halves
    return pl.pallas_call(
        project_body,
        out_shape=jax.ShapeDtypeStruct((blocks, rows, cut), BF16),
        grid_spec=pltpu.PrefetchScalarGridSpec(
            num_scalar_prefetch=1,
            grid=(blocks, halves),
            in_specs=[
                pl.BlockSpec((rows, depth), lambda q, j, m: (0, 0)),
                pl.BlockSpec((depth, step), lambda q, j, m: (0, q * halves + j)),
                pl.BlockSpec((own, step), lambda q, j, m: (0, q * halves + j)),
            ],
            out_specs=pl.BlockSpec((1, rows, step), lambda q, j, m: (q, 0, j)),
            scratch_shapes=[pltpu.VMEM((rows, step), F32)],
        ),
        compiler_params=pltpu.CompilerParams(vmem_limit_bytes=56 << 20),
        cost_estimate=pl.CostEstimate(
            flops=2 * rows * depth * width,
            bytes_accessed=2 * (rows * depth + depth * width + rows * width),
            transcendentals=0,
        ),
    )(mine, context, weight, residual)


def first_body(a_ref, gain_ref, w_ref, g_ref, s_ref, o_ref):
    depth = a_ref.shape[1]
    h = w_ref.shape[1]
    squares = None
    for at in range(0, depth, 256):
        wide = a_ref[:, at : at + 256].astype(F32)
        for i in range(0, 256, 128):
            part = wide[:, i : i + 128]
            squares = part * part if squares is None else squares + part * part
        g_ref[:, at : at + 256] = (wide * gain_ref[:, at : at + 256]).astype(BF16)
    gained = g_ref[...]
    for i in range(2):
        o_ref[:, i * h : (i + 1) * h] = jnp.dot(
            gained, w_ref[i * depth : (i + 1) * depth, :], preferred_element_type=F32
        ).astype(BF16)
    s_ref[...] = jnp.sum(squares, axis=1, keepdims=True)


WHOLE = pl.BlockSpec(memory_space=pltpu.VMEM)


def first_product(arrived, gain, weight):
    rows, depth = arrived.shape
    cols = 2 * weight.shape[1]
    return pl.pallas_call(
        first_body,
        out_shape=(
            jax.ShapeDtypeStruct((rows, depth), BF16),
            jax.ShapeDtypeStruct((rows, 1), F32),
            jax.ShapeDtypeStruct((rows, cols), BF16),
        ),
        in_specs=[WHOLE] * 3,
        out_specs=(WHOLE,) * 3,
        compiler_params=pltpu.CompilerParams(vmem_limit_bytes=32 << 20),
        cost_estimate=pl.CostEstimate(
            flops=2 * rows * depth * cols,
            bytes_accessed=2 * (2 * rows * depth + depth * cols + rows * cols),
            transcendentals=0,
        ),
    )(arrived, gain, weight)


def down_body(start, *refs):
    own, from_mate, from_twin, from_far, w_own, w_mate, w_twin, w_far, w_rest, o_ref = refs
    h = own.shape[1]
    for j in range(o_ref.shape[1] // h):
        cols = slice(j * h, (j + 1) * h)
        at = slice(start + j * h, start + (j + 1) * h)
        total = jnp.dot(own[...], w_own[:, cols], preferred_element_type=F32)
        total += jnp.dot(from_mate[...], w_mate[at, :], preferred_element_type=F32)
        total += jnp.dot(from_twin[...], w_twin[:, cols], preferred_element_type=F32)
        there = j * h - w_far.shape[0]
        far = w_far[cols, :] if there < 0 else w_rest[there : there + h, :]
        total += jnp.dot(from_far[...], far, preferred_element_type=F32)
        o_ref[:, cols] = total.astype(BF16)


def down_product(blocks, weights, start):
    rows, h = blocks[0].shape
    cols = weights[0].shape[1]
    return pl.pallas_call(
        functools.partial(down_body, start),
        out_shape=jax.ShapeDtypeStruct((rows, cols), BF16),
        in_specs=[WHOLE] * 9,
        out_specs=WHOLE,
        compiler_params=pltpu.CompilerParams(vmem_limit_bytes=32 << 20),
        cost_estimate=pl.CostEstimate(
            flops=8 * rows * h * cols,
            bytes_accessed=2 * (4 * rows * h + 4 * h * cols + rows * cols),
            transcendentals=0,
        ),
    )(*blocks, *weights)


def bundle_body(at_ref, g_ref, u_ref, d_ref, o_ref):
    step = pl.program_id(0)
    h = o_ref.shape[1]

    @pl.when(step < 2)
    def _():
        o_ref[...] = g_ref[0]

    @pl.when((step >= 2) & (step < 4))
    def _():
        o_ref[...] = u_ref[0]

    @pl.when(step >= 4)
    def _():
        for j in range(d_ref.shape[2] // h):
            o_ref[j * h : (j + 1) * h, :] = d_ref[0, :, j * h : (j + 1) * h]


def bundle(at, gate, up, down):
    deep, h = gate.shape[1:]
    cut = deep // 4

    def pick(last_first):
        return lambda i, at: at[jnp.where(i <= last_first, 0, 1)]

    gate_at, up_at, down_at = pick(0), pick(2), pick(4)
    return pl.pallas_call(
        bundle_body,
        out_shape=jax.ShapeDtypeStruct((6 * cut, h), BF16),
        grid_spec=pltpu.PrefetchScalarGridSpec(
            num_scalar_prefetch=1,
            grid=(6,),
            in_specs=[
                pl.BlockSpec((1, cut, h), lambda i, at: (0, gate_at(i, at), 0)),
                pl.BlockSpec((1, cut, h), lambda i, at: (0, up_at(i, at), 0)),
                pl.BlockSpec((1, h, cut), lambda i, at: (0, 0, down_at(i, at))),
            ],
            out_specs=pl.BlockSpec((cut, h), lambda i, at: (i, 0)),
        ),
        compiler_params=pltpu.CompilerParams(vmem_limit_bytes=56 << 20),
        cost_estimate=pl.CostEstimate(
            flops=0, bytes_accessed=24 * cut * h, transcendentals=0
        ),
    )(at, gate, up, down)


def pack_body(at_ref, g_ref, u_ref, o_ref):
    h = g_ref.shape[2]
    o_ref[:, :h] = g_ref[0]
    o_ref[:, h:] = u_ref[0]


def pack(at, gate, up):
    deep, h = gate.shape[1:]
    cut = deep // 4
    steps = at.shape[0]
    return pl.pallas_call(
        pack_body,
        out_shape=jax.ShapeDtypeStruct((steps * cut, 2 * h), BF16),
        grid_spec=pltpu.PrefetchScalarGridSpec(
            num_scalar_prefetch=1,
            grid=(steps,),
            in_specs=[
                pl.BlockSpec((1, cut, h), lambda i, at: (0, at[i], 0)),
                pl.BlockSpec((1, cut, h), lambda i, at: (0, at[i], 0)),
            ],
            out_specs=pl.BlockSpec((cut, 2 * h), lambda i, at: (i, 0)),
        ),
        compiler_params=pltpu.CompilerParams(vmem_limit_bytes=56 << 20),
        cost_estimate=pl.CostEstimate(
            flops=0, bytes_accessed=8 * steps * cut * h, transcendentals=0
        ),
    )(at, gate, up)


def local(context, out_proj, residual, norm_gain, expert_ids, gates, gate_proj, up_proj, down_proj):
    ny, nc, nz, nx = (lax.axis_size(a) for a in ("y", "c", "z", "x"))
    rows_here, width = residual.shape
    quarter = width // nx
    experts_total = ny * nc * nz
    capacity = min(rows_here, max(2, rows_here * TOPK * 5 // (4 * experts_total)))
    x = lax.axis_index("x")
    c = lax.axis_index("c")
    mate = jnp.where(c == 0, x ^ 1, x ^ 3)
    twin = jnp.where(c == 0, x ^ 3, x ^ 1)
    tokens_core = nx * rows_here
    tokens = nc * tokens_core

    to_mate = lambda value: from_places(value, lambda c, x: (c, mate_of(c, x)))
    to_twin = lambda value: from_places(value, lambda c, x: (c, twin_of(c, x)))

    def cut_down(at):
        return lax.dynamic_slice(
            down_proj[0], (0, at * quarter), (down_proj.shape[1], quarter)
        )

    twin_cut, context = lax.optimization_barrier((cut_down(twin), context))
    twin_down = to_twin(twin_cut)

    mine = lax.axis_index("z") * nx + x
    part = project(mine[None].astype(jnp.int32), context, out_proj, residual, nx)

    meta = jnp.concatenate([expert_ids.astype(BF16), gates], axis=1)
    meta = jnp.pad(meta, ((0, 0), (0, 128 - meta.shape[1])))
    came = [meta] + [shift(meta, "x", k) for k in range(1, nx)]
    part, came, twin_down, down_proj = lax.optimization_barrier((part, came, twin_down, down_proj))
    part = exchange(part.reshape(nx * nz, tokens_core, quarter), ("x", "z"))
    ring = [came[(nx - m) % nx] for m in range(nx)]
    ring = jnp.concatenate(ring + ring[:-1], axis=0)
    meta_own = lax.dynamic_slice(
        ring, (lax.rem(nx - x, nx) * rows_here, jnp.int32(0)), (tokens_core, meta.shape[1])
    )
    meta_all = jnp.concatenate([meta_own, shift(meta_own, "c", 1)], axis=0)
    ids = meta_all[:, :TOPK].astype(jnp.int32)
    gate_vals = meta_all[:, TOPK : 2 * TOPK].astype(F32)

    places = ny * nz
    place = jnp.arange(places, dtype=jnp.int32)
    expert_of = ((place // nz) * nc + c) * nz + lax.rem(place, nz)
    matches = ids[:, :, None] == expert_of[None, None, :]
    picked = jnp.any(matches, axis=1).astype(jnp.int32)
    weighted = jnp.sum(jnp.where(matches, gate_vals[:, :, None], F32(0)), axis=1)
    by_device = picked.reshape(nc * nx, rows_here, places)
    ranking = jnp.cumsum(by_device, axis=1) - by_device
    admitted = (by_device > 0) & (ranking < capacity)
    device_iota = jnp.arange(nc * nx, dtype=jnp.int32)[:, None, None]
    slot = jnp.where(admitted, device_iota * capacity + ranking, -1).reshape(tokens, places)
    slots = nc * nx * capacity
    slot_iota = jnp.arange(slots, dtype=jnp.int32)
    chosen = slot.T[:, None, :] == slot_iota[None, :, None]
    selector = chosen.astype(BF16).reshape(places * slots, tokens)
    scaled = jnp.where(chosen, weighted.T[:, None, :], F32(0)).astype(BF16)
    scaled = scaled.reshape(places * slots, tokens)
    kept = pack(jnp.stack([x, twin]).astype(jnp.int32), gate_proj, up_proj)
    given = bundle(jnp.stack([mate, x ^ 2]).astype(jnp.int32), gate_proj, up_proj, down_proj)
    own_down = cut_down(x)
    gain = jnp.concatenate(
        [lax.dynamic_slice(norm_gain, (q * quarter,), (quarter,)) for q in (x, twin)]
    )[None, :]
    selector, scaled, part, kept, given, own_down, gain = lax.optimization_barrier(
        (selector, scaled, part, kept, given, own_down, gain)
    )

    hidden = jnp.sum(part.astype(F32), axis=0).astype(BF16)
    hidden_wide = hidden.astype(F32)

    twin_own = from_places(hidden, lambda c, x: (c, twin_of(c, x)))
    near_other = from_places(hidden, lambda c, x: (1 - c, x))
    twin_other = from_places(hidden, lambda c, x: (1 - c, twin_of(c, x)))
    twin_own, near_other, twin_other, given = lax.optimization_barrier(
        (twin_own, near_other, twin_other, given)
    )
    rows = jnp.concatenate(
        [
            jnp.concatenate([hidden, near_other], axis=0),
            jnp.concatenate([twin_own, twin_other], axis=0),
        ],
        axis=1,
    )
    outgoing = jnp.dot(selector, rows, preferred_element_type=F32).astype(BF16)
    arrived = exchange(outgoing.reshape(places, slots, 2 * quarter), ("y", "z"))
    arrived = arrived.reshape(places * slots, 2 * quarter)

    taken = to_mate(given)
    arrived, taken = lax.optimization_barrier((arrived, taken))
    deep = taken.shape[0] // 6
    early = 5 * deep + EARLY * gate_proj.shape[2]
    arrived, far_down, far_rest = lax.optimization_barrier(
        (arrived, taken[5 * deep : early], taken[early:])
    )
    far_down = to_twin(far_down)
    gained, square, theirs = first_product(arrived, gain, taken)
    came_back = to_mate(theirs)
    inverse = lax.rsqrt((square + to_mate(square)) / width + 1e-06)
    total = jnp.dot(gained, kept, preferred_element_type=F32)
    total, came_back, far_down, far_rest = lax.optimization_barrier(
        (total, came_back, far_down, far_rest)
    )
    far_rest = to_twin(far_rest)
    total = total + came_back.astype(F32)
    total = total * inverse
    hid = total.shape[1] // 2
    activated = (jax.nn.silu(total[:, :hid]) * total[:, hid:]).astype(BF16)
    blocks = (activated, to_mate(activated), to_twin(activated), shift(activated, "x", 2))
    result = down_product(blocks, (own_down, taken, twin_down, far_down, far_rest), 4 * deep)

    returned = exchange(result.reshape(places, slots, quarter), ("y", "z"))
    returned = returned.reshape(places * slots, quarter)
    mixture = lax.dot_general(
        scaled, returned, (((0,), (0,)), ((), ())), preferred_element_type=F32
    )
    mixture = mixture[:tokens_core] + shift(mixture[tokens_core:], "c", 1)
    out = (hidden_wide + mixture).astype(BF16)
    out = exchange(out.reshape(nx, rows_here, quarter), "x")
    return out.transpose(1, 0, 2).reshape(rows_here, width)


def solution(mesh):
    grid = Mesh(mesh.devices.reshape(4, 2, 4, 4), ("y", "c", "z", "x"))
    group, member = ("y", "c"), ("z", "x")
    owner = group + member
    in_specs = (
        P(group, member),
        P(member, None),
        P(owner, None),
        P(),
        P(owner, None),
        P(owner, None),
        P(owner, None, None),
        P(owner, None, None),
        P(owner, None, None),
    )
    return jax.shard_map(
        local, mesh=grid, in_specs=in_specs, out_specs=P(owner, None), check_vma=False
    )
```

```python
import functools

import jax
import jax.numpy as jnp
from jax import lax
from jax.experimental import pallas as pl
from jax.experimental.pallas import tpu as pltpu
from jax.sharding import Mesh
from jax.sharding import PartitionSpec as P

TOPK = 8
F32 = jnp.float32
BF16 = jnp.bfloat16


def shift(value, axis, amount):
    size = lax.axis_size(axis)
    return lax.ppermute(value, axis, [(i, (i + amount) % size) for i in range(size)])


def exchange(value, axes):
    return lax.all_to_all(value, axes, split_axis=0, concat_axis=0, tiled=True)


def mate_of(c, x):
    return x ^ 1 if c == 0 else x ^ 3


def twin_of(c, x):
    return x ^ 3 if c == 0 else x ^ 1


def from_places(value, source):
    pairs = []
    for c in range(2):
        for x in range(4):
            sc, sx = source(c, x)
            pairs.append((sc * 4 + sx, c * 4 + x))
    return lax.ppermute(value, ("c", "x"), pairs)


def project_body(mine_ref, a_ref, b_ref, r_ref, o_ref, acc_ref):
    own = r_ref.shape[0]
    acc_ref[...] = jnp.dot(a_ref[...], b_ref[...], preferred_element_type=F32)
    here = pl.ds(pl.multiple_of(mine_ref[0] * own, own), own)
    acc_ref[here, :] += r_ref[...].astype(F32)
    o_ref[...] = acc_ref[...].astype(BF16)


def project(mine, context, weight, residual, blocks):
    rows, depth = context.shape
    own, width = residual.shape
    step = width // blocks
    return pl.pallas_call(
        project_body,
        out_shape=jax.ShapeDtypeStruct((rows, width), BF16),
        grid_spec=pltpu.PrefetchScalarGridSpec(
            num_scalar_prefetch=1,
            grid=(blocks,),
            in_specs=[
                pl.BlockSpec((rows, depth), lambda q, m: (0, 0)),
                pl.BlockSpec((depth, step), lambda q, m: (0, q)),
                pl.BlockSpec((own, step), lambda q, m: (0, q)),
            ],
            out_specs=pl.BlockSpec((rows, step), lambda q, m: (0, q)),
            scratch_shapes=[pltpu.VMEM((rows, step), F32)],
        ),
        compiler_params=pltpu.CompilerParams(vmem_limit_bytes=56 << 20),
        cost_estimate=pl.CostEstimate(
            flops=2 * rows * depth * width,
            bytes_accessed=2 * (rows * depth + depth * width + rows * width),
            transcendentals=0,
        ),
    )(mine, context, weight, residual)


def gather_sum_body(a_ref, o_ref):
    total = a_ref[0].astype(F32)
    for i in range(1, a_ref.shape[0]):
        total += a_ref[i].astype(F32)
    o_ref[0] = total.astype(BF16)


def gather_sum(terms, blocks):
    count, rows, width = terms.shape
    step = width // blocks
    return pl.pallas_call(
        gather_sum_body,
        out_shape=jax.ShapeDtypeStruct((blocks, rows, step), BF16),
        grid=(blocks,),
        in_specs=[pl.BlockSpec((count, rows, step), lambda q: (0, 0, q))],
        out_specs=pl.BlockSpec((1, rows, step), lambda q: (q, 0, 0)),
        compiler_params=pltpu.CompilerParams(vmem_limit_bytes=24 << 20),
        cost_estimate=pl.CostEstimate(
            flops=count * rows * width,
            bytes_accessed=2 * (count + 1) * rows * width,
            transcendentals=0,
        ),
    )(terms)


def first_body(a_ref, gain_ref, w_ref, g_ref, s_ref, o_ref):
    depth = a_ref.shape[1]
    h = w_ref.shape[1]
    squares = None
    for at in range(0, depth, 256):
        wide = a_ref[:, at : at + 256].astype(F32)
        for i in range(0, 256, 128):
            part = wide[:, i : i + 128]
            squares = part * part if squares is None else squares + part * part
        g_ref[:, at : at + 256] = (wide * gain_ref[:, at : at + 256]).astype(BF16)
    gained = g_ref[...]
    for i in range(2):
        o_ref[:, i * h : (i + 1) * h] = jnp.dot(
            gained, w_ref[i * depth : (i + 1) * depth, :], preferred_element_type=F32
        ).astype(BF16)
    s_ref[...] = jnp.sum(squares, axis=1, keepdims=True)


WHOLE = pl.BlockSpec(memory_space=pltpu.VMEM)


def first_product(arrived, gain, weight):
    rows, depth = arrived.shape
    cols = 2 * weight.shape[1]
    return pl.pallas_call(
        first_body,
        out_shape=(
            jax.ShapeDtypeStruct((rows, depth), BF16),
            jax.ShapeDtypeStruct((rows, 1), F32),
            jax.ShapeDtypeStruct((rows, cols), BF16),
        ),
        in_specs=[WHOLE] * 3,
        out_specs=(WHOLE,) * 3,
        compiler_params=pltpu.CompilerParams(vmem_limit_bytes=32 << 20),
        cost_estimate=pl.CostEstimate(
            flops=2 * rows * depth * cols,
            bytes_accessed=2 * (2 * rows * depth + depth * cols + rows * cols),
            transcendentals=0,
        ),
    )(arrived, gain, weight)


def down_body(start, *refs):
    own, from_mate, from_twin, from_far, w_own, w_mate, w_twin, w_far, o_ref = refs
    h = own.shape[1]
    for j in range(o_ref.shape[1] // h):
        cols = slice(j * h, (j + 1) * h)
        at = slice(start + j * h, start + (j + 1) * h)
        total = jnp.dot(own[...], w_own[:, cols], preferred_element_type=F32)
        total += jnp.dot(from_mate[...], w_mate[at, :], preferred_element_type=F32)
        total += jnp.dot(from_twin[...], w_twin[:, cols], preferred_element_type=F32)
        total += jnp.dot(from_far[...], w_far[:, cols], preferred_element_type=F32)
        o_ref[:, cols] = total.astype(BF16)


def down_product(blocks, weights, start):
    rows, h = blocks[0].shape
    cols = weights[0].shape[1]
    return pl.pallas_call(
        functools.partial(down_body, start),
        out_shape=jax.ShapeDtypeStruct((rows, cols), BF16),
        in_specs=[WHOLE] * 8,
        out_specs=WHOLE,
        compiler_params=pltpu.CompilerParams(vmem_limit_bytes=32 << 20),
        cost_estimate=pl.CostEstimate(
            flops=8 * rows * h * cols,
            bytes_accessed=2 * (4 * rows * h + 4 * h * cols + rows * cols),
            transcendentals=0,
        ),
    )(*blocks, *weights)


def bundle_body(at_ref, g_ref, u_ref, d_ref, o_ref):
    step = pl.program_id(0)
    h = o_ref.shape[1]

    @pl.when(step < 2)
    def _():
        o_ref[...] = g_ref[0]

    @pl.when((step >= 2) & (step < 4))
    def _():
        o_ref[...] = u_ref[0]

    @pl.when(step >= 4)
    def _():
        for j in range(d_ref.shape[2] // h):
            o_ref[j * h : (j + 1) * h, :] = d_ref[0, :, j * h : (j + 1) * h]


def bundle(at, gate, up, down):
    deep, h = gate.shape[1:]
    cut = deep // 4

    gate_at = lambda i, at: at[jnp.where(i <= 0, 0, 1)]
    up_at = lambda i, at: at[jnp.where(i <= 2, 0, 1)]
    return pl.pallas_call(
        bundle_body,
        out_shape=jax.ShapeDtypeStruct((5 * cut, h), BF16),
        grid_spec=pltpu.PrefetchScalarGridSpec(
            num_scalar_prefetch=1,
            grid=(5,),
            in_specs=[
                pl.BlockSpec((1, cut, h), lambda i, at: (0, gate_at(i, at), 0)),
                pl.BlockSpec((1, cut, h), lambda i, at: (0, up_at(i, at), 0)),
                pl.BlockSpec((1, h, cut), lambda i, at: (0, 0, at[0])),
            ],
            out_specs=pl.BlockSpec((cut, h), lambda i, at: (i, 0)),
        ),
        compiler_params=pltpu.CompilerParams(vmem_limit_bytes=56 << 20),
        cost_estimate=pl.CostEstimate(
            flops=0, bytes_accessed=20 * cut * h, transcendentals=0
        ),
    )(at, gate, up, down)


def pack_body(at_ref, g_ref, u_ref, o_ref):
    h = g_ref.shape[2]
    o_ref[:, :h] = g_ref[0]
    o_ref[:, h:] = u_ref[0]


def pack(at, gate, up):
    deep, h = gate.shape[1:]
    cut = deep // 4
    steps = at.shape[0]
    return pl.pallas_call(
        pack_body,
        out_shape=jax.ShapeDtypeStruct((steps * cut, 2 * h), BF16),
        grid_spec=pltpu.PrefetchScalarGridSpec(
            num_scalar_prefetch=1,
            grid=(steps,),
            in_specs=[
                pl.BlockSpec((1, cut, h), lambda i, at: (0, at[i], 0)),
                pl.BlockSpec((1, cut, h), lambda i, at: (0, at[i], 0)),
            ],
            out_specs=pl.BlockSpec((cut, 2 * h), lambda i, at: (i, 0)),
        ),
        compiler_params=pltpu.CompilerParams(vmem_limit_bytes=56 << 20),
        cost_estimate=pl.CostEstimate(
            flops=0, bytes_accessed=8 * steps * cut * h, transcendentals=0
        ),
    )(at, gate, up)


def local(context, out_proj, residual, norm_gain, expert_ids, gates, gate_proj, up_proj, down_proj):
    ny, nc, nz, nx = (lax.axis_size(a) for a in ("y", "c", "z", "x"))
    rows_here, width = residual.shape
    quarter = width // nx
    experts_total = ny * nc * nz
    capacity = min(rows_here, max(2, rows_here * TOPK * 5 // (4 * experts_total)))
    x = lax.axis_index("x")
    c = lax.axis_index("c")
    mate = jnp.where(c == 0, x ^ 1, x ^ 3)
    twin = jnp.where(c == 0, x ^ 3, x ^ 1)
    tokens_core = nx * rows_here
    tokens = nc * tokens_core

    to_mate = lambda value: from_places(value, lambda c, x: (c, mate_of(c, x)))
    to_twin = lambda value: from_places(value, lambda c, x: (c, twin_of(c, x)))

    def cut_down(at):
        return lax.dynamic_slice(
            down_proj[0], (0, at * quarter), (down_proj.shape[1], quarter)
        )

    mine = lax.axis_index("z") * nx + x
    part = project(mine[None].astype(jnp.int32), context, out_proj, residual, nx)

    meta = jnp.concatenate([expert_ids.astype(BF16), gates], axis=1)
    meta = jnp.pad(meta, ((0, 0), (0, 128 - meta.shape[1])))
    came = [meta] + [shift(meta, "x", k) for k in range(1, nx)]
    part = exchange(part.reshape(nz, tokens_core, width), "z")
    ring = [came[(nx - m) % nx] for m in range(nx)]
    ring = jnp.concatenate(ring + ring[:-1], axis=0)
    meta_own = lax.dynamic_slice(
        ring, (lax.rem(nx - x, nx) * rows_here, jnp.int32(0)), (tokens_core, meta.shape[1])
    )
    meta_all = jnp.concatenate([meta_own, shift(meta_own, "c", 1)], axis=0)
    ids = meta_all[:, :TOPK].astype(jnp.int32)
    gate_vals = meta_all[:, TOPK : 2 * TOPK].astype(F32)

    places = ny * nz
    place = jnp.arange(places, dtype=jnp.int32)
    expert_of = ((place // nz) * nc + c) * nz + lax.rem(place, nz)
    matches = ids[:, :, None] == expert_of[None, None, :]
    picked = jnp.any(matches, axis=1).astype(jnp.int32)
    weighted = jnp.sum(jnp.where(matches, gate_vals[:, :, None], F32(0)), axis=1)
    by_device = picked.reshape(nc * nx, rows_here, places)
    ranking = jnp.cumsum(by_device, axis=1) - by_device
    admitted = (by_device > 0) & (ranking < capacity)
    device_iota = jnp.arange(nc * nx, dtype=jnp.int32)[:, None, None]
    slot = jnp.where(admitted, device_iota * capacity + ranking, -1).reshape(tokens, places)
    slots = nc * nx * capacity
    slot_iota = jnp.arange(slots, dtype=jnp.int32)
    chosen = slot.T[:, None, :] == slot_iota[None, :, None]
    selector = chosen.astype(BF16).reshape(places * slots, tokens)
    scaled = jnp.where(chosen, weighted.T[:, None, :], F32(0)).astype(BF16)
    scaled = scaled.reshape(places * slots, tokens)
    kept = pack(jnp.stack([x, twin]).astype(jnp.int32), gate_proj, up_proj)
    given = bundle(jnp.stack([mate, x ^ 2]).astype(jnp.int32), gate_proj, up_proj, down_proj)
    own_down, twin_cut, far_cut = cut_down(x), cut_down(twin), cut_down(x ^ 2)
    twin_down = to_twin(twin_cut)
    far_down = to_twin(to_mate(far_cut))
    gain = jnp.concatenate(
        [lax.dynamic_slice(norm_gain, (q * quarter,), (quarter,)) for q in (x, twin)]
    )[None, :]
    selector, scaled, part, kept, given, own_down, gain, twin_down, far_down = (
        lax.optimization_barrier(
            (selector, scaled, part, kept, given, own_down, gain, twin_down, far_down)
        )
    )
    part = exchange(gather_sum(part, nx), "x")

    hidden = jnp.sum(part.astype(F32), axis=0).astype(BF16)
    hidden_wide = hidden.astype(F32)

    twin_own = from_places(hidden, lambda c, x: (c, twin_of(c, x)))
    near_other = from_places(hidden, lambda c, x: (1 - c, x))
    twin_other = from_places(hidden, lambda c, x: (1 - c, twin_of(c, x)))
    twin_own, near_other, twin_other, given = lax.optimization_barrier(
        (twin_own, near_other, twin_other, given)
    )
    rows = jnp.concatenate(
        [
            jnp.concatenate([hidden, near_other], axis=0),
            jnp.concatenate([twin_own, twin_other], axis=0),
        ],
        axis=1,
    )
    outgoing = jnp.dot(selector, rows, preferred_element_type=F32).astype(BF16)
    arrived = exchange(outgoing.reshape(places, slots, 2 * quarter), ("y", "z"))
    arrived = arrived.reshape(places * slots, 2 * quarter)

    taken = to_mate(given)
    arrived, taken = lax.optimization_barrier((arrived, taken))
    gained, square, theirs = first_product(arrived, gain, taken)
    came_back = to_mate(theirs)
    inverse = lax.rsqrt((square + to_mate(square)) / width + 1e-06)
    total = jnp.dot(gained, kept, preferred_element_type=F32)
    total, came_back = lax.optimization_barrier((total, came_back))
    total = total + came_back.astype(F32)
    total = total * inverse
    hid = total.shape[1] // 2
    activated = (jax.nn.silu(total[:, :hid]) * total[:, hid:]).astype(BF16)
    blocks = (activated, to_mate(activated), to_twin(activated), shift(activated, "x", 2))
    result = down_product(blocks, (own_down, taken, twin_down, far_down), 4 * quarter)

    returned = exchange(result.reshape(places, slots, quarter), ("y", "z"))
    returned = returned.reshape(places * slots, quarter)
    mixture = lax.dot_general(
        scaled, returned, (((0,), (0,)), ((), ())), preferred_element_type=F32
    )
    mixture = mixture[:tokens_core] + shift(mixture[tokens_core:], "c", 1)
    out = (hidden_wide + mixture).astype(BF16)
    out = exchange(out.reshape(nx, rows_here, quarter), "x")
    return out.transpose(1, 0, 2).reshape(rows_here, width)


def solution(mesh):
    grid = Mesh(mesh.devices.reshape(4, 2, 4, 4), ("y", "c", "z", "x"))
    group, member = ("y", "c"), ("z", "x")
    owner = group + member
    in_specs = (
        P(group, member),
        P(member, None),
        P(owner, None),
        P(),
        P(owner, None),
        P(owner, None),
        P(owner, None, None),
        P(owner, None, None),
        P(owner, None, None),
    )
    return jax.shard_map(
        local, mesh=grid, in_specs=in_specs, out_specs=P(owner, None), check_vma=False
    )
```

```python
import functools

import jax
import jax.numpy as jnp
from jax import lax
from jax.experimental import pallas as pl
from jax.experimental.pallas import tpu as pltpu
from jax.sharding import Mesh
from jax.sharding import PartitionSpec as P

TOPK = 8
F32 = jnp.float32
BF16 = jnp.bfloat16


def shift(value, axis, amount):
    size = lax.axis_size(axis)
    return lax.ppermute(value, axis, [(i, (i + amount) % size) for i in range(size)])


def exchange(value, axes):
    return lax.all_to_all(value, axes, split_axis=0, concat_axis=0, tiled=True)


def mate_of(c, x):
    return x ^ 1 if c == 0 else x ^ 3


def twin_of(c, x):
    return x ^ 3 if c == 0 else x ^ 1


def from_places(value, source):
    pairs = []
    for c in range(2):
        for x in range(4):
            sc, sx = source(c, x)
            pairs.append((sc * 4 + sx, c * 4 + x))
    return lax.ppermute(value, ("c", "x"), pairs)


def project_body(a_ref, b_ref, o_ref):
    o_ref[...] = jnp.dot(a_ref[...], b_ref[...], preferred_element_type=F32).astype(BF16)


def project(context, weight, blocks):
    rows, depth = context.shape
    width = weight.shape[1]
    step = width // blocks
    return pl.pallas_call(
        project_body,
        out_shape=jax.ShapeDtypeStruct((rows, width), BF16),
        grid=(blocks,),
        in_specs=[
            pl.BlockSpec((rows, depth), lambda q: (0, 0)),
            pl.BlockSpec((depth, step), lambda q: (0, q)),
        ],
        out_specs=pl.BlockSpec((rows, step), lambda q: (0, q)),
        compiler_params=pltpu.CompilerParams(vmem_limit_bytes=56 << 20),
        cost_estimate=pl.CostEstimate(
            flops=2 * rows * depth * width,
            bytes_accessed=2 * (rows * depth + depth * width + rows * width),
            transcendentals=0,
        ),
    )(context, weight)


def owner_sum_body(at_ref, a_ref, r_ref, *refs):
    outs, acc_ref = refs[:-1], refs[-1]
    step = pl.program_id(0)
    own = r_ref.shape[0]
    total = a_ref[0].astype(F32)
    for i in range(1, a_ref.shape[0]):
        total += a_ref[i].astype(F32)
    acc_ref[...] = total
    here = pl.ds(pl.multiple_of(at_ref[0] * own, own), own)
    acc_ref[here, :] += r_ref[...].astype(F32)
    for k, o_ref in enumerate(outs):

        @pl.when(step == k)
        def _():
            o_ref[...] = acc_ref[...].astype(BF16)


def owner_sum(at, terms, residual, blocks):
    count, rows, width = terms.shape
    step = width // blocks
    turn = lambda q, at: lax.rem(at[0] + q, blocks)
    return pl.pallas_call(
        owner_sum_body,
        out_shape=[jax.ShapeDtypeStruct((rows, step), BF16)] * blocks,
        grid_spec=pltpu.PrefetchScalarGridSpec(
            num_scalar_prefetch=1,
            grid=(blocks,),
            in_specs=[
                pl.BlockSpec((count, rows, step), lambda q, at: (0, 0, turn(q, at))),
                pl.BlockSpec((residual.shape[0], step), lambda q, at: (0, turn(q, at))),
            ],
            out_specs=[pl.BlockSpec((rows, step), lambda q, at: (0, 0))] * blocks,
            scratch_shapes=[pltpu.VMEM((rows, step), F32)],
        ),
        compiler_params=pltpu.CompilerParams(vmem_limit_bytes=24 << 20),
        cost_estimate=pl.CostEstimate(
            flops=count * rows * width,
            bytes_accessed=2 * (count + 1) * rows * width,
            transcendentals=0,
        ),
    )(at, terms, residual)


def first_body(a_ref, gain_ref, w_ref, g_ref, s_ref, o_ref):
    depth = a_ref.shape[1]
    h = w_ref.shape[1]
    squares = None
    for at in range(0, depth, 256):
        wide = a_ref[:, at : at + 256].astype(F32)
        for i in range(0, 256, 128):
            part = wide[:, i : i + 128]
            squares = part * part if squares is None else squares + part * part
        g_ref[:, at : at + 256] = (wide * gain_ref[:, at : at + 256]).astype(BF16)
    gained = g_ref[...]
    for i in range(2):
        o_ref[:, i * h : (i + 1) * h] = jnp.dot(
            gained, w_ref[i * depth : (i + 1) * depth, :], preferred_element_type=F32
        ).astype(BF16)
    s_ref[...] = jnp.sum(squares, axis=1, keepdims=True)


WHOLE = pl.BlockSpec(memory_space=pltpu.VMEM)


def first_product(arrived, gain, weight):
    rows, depth = arrived.shape
    cols = 2 * weight.shape[1]
    return pl.pallas_call(
        first_body,
        out_shape=(
            jax.ShapeDtypeStruct((rows, depth), BF16),
            jax.ShapeDtypeStruct((rows, 1), F32),
            jax.ShapeDtypeStruct((rows, cols), BF16),
        ),
        in_specs=[WHOLE] * 3,
        out_specs=(WHOLE,) * 3,
        compiler_params=pltpu.CompilerParams(vmem_limit_bytes=32 << 20),
        cost_estimate=pl.CostEstimate(
            flops=2 * rows * depth * cols,
            bytes_accessed=2 * (2 * rows * depth + depth * cols + rows * cols),
            transcendentals=0,
        ),
    )(arrived, gain, weight)


def down_body(start, *refs):
    own, from_mate, from_twin, from_far, w_own, w_mate, w_twin, w_far, o_ref = refs
    h = own.shape[1]
    for j in range(o_ref.shape[1] // h):
        cols = slice(j * h, (j + 1) * h)
        at = slice(start + j * h, start + (j + 1) * h)
        total = jnp.dot(own[...], w_own[:, cols], preferred_element_type=F32)
        total += jnp.dot(from_mate[...], w_mate[at, :], preferred_element_type=F32)
        total += jnp.dot(from_twin[...], w_twin[:, cols], preferred_element_type=F32)
        total += jnp.dot(from_far[...], w_far[:, cols], preferred_element_type=F32)
        o_ref[:, cols] = total.astype(BF16)


def down_product(blocks, weights, start):
    rows, h = blocks[0].shape
    cols = weights[0].shape[1]
    return pl.pallas_call(
        functools.partial(down_body, start),
        out_shape=jax.ShapeDtypeStruct((rows, cols), BF16),
        in_specs=[WHOLE] * 8,
        out_specs=WHOLE,
        compiler_params=pltpu.CompilerParams(vmem_limit_bytes=32 << 20),
        cost_estimate=pl.CostEstimate(
            flops=8 * rows * h * cols,
            bytes_accessed=2 * (4 * rows * h + 4 * h * cols + rows * cols),
            transcendentals=0,
        ),
    )(*blocks, *weights)


def bundle_body(at_ref, g_ref, u_ref, d_ref, o_ref):
    step = pl.program_id(0)
    h = o_ref.shape[1]

    @pl.when(step < 2)
    def _():
        o_ref[...] = g_ref[0]

    @pl.when((step >= 2) & (step < 4))
    def _():
        o_ref[...] = u_ref[0]

    @pl.when(step >= 4)
    def _():
        for j in range(d_ref.shape[2] // h):
            o_ref[j * h : (j + 1) * h, :] = d_ref[0, :, j * h : (j + 1) * h]


def bundle(at, gate, up, down):
    deep, h = gate.shape[1:]
    cut = deep // 4

    gate_at = lambda i, at: at[jnp.where(i <= 0, 0, 1)]
    up_at = lambda i, at: at[jnp.where(i <= 2, 0, 1)]
    return pl.pallas_call(
        bundle_body,
        out_shape=jax.ShapeDtypeStruct((5 * cut, h), BF16),
        grid_spec=pltpu.PrefetchScalarGridSpec(
            num_scalar_prefetch=1,
            grid=(5,),
            in_specs=[
                pl.BlockSpec((1, cut, h), lambda i, at: (0, gate_at(i, at), 0)),
                pl.BlockSpec((1, cut, h), lambda i, at: (0, up_at(i, at), 0)),
                pl.BlockSpec((1, h, cut), lambda i, at: (0, 0, at[0])),
            ],
            out_specs=pl.BlockSpec((cut, h), lambda i, at: (i, 0)),
        ),
        compiler_params=pltpu.CompilerParams(vmem_limit_bytes=56 << 20),
        cost_estimate=pl.CostEstimate(
            flops=0, bytes_accessed=20 * cut * h, transcendentals=0
        ),
    )(at, gate, up, down)


def pack_body(at_ref, g_ref, u_ref, o_ref):
    h = g_ref.shape[2]
    o_ref[:, :h] = g_ref[0]
    o_ref[:, h:] = u_ref[0]


def pack(at, gate, up):
    deep, h = gate.shape[1:]
    cut = deep // 4
    steps = at.shape[0]
    return pl.pallas_call(
        pack_body,
        out_shape=jax.ShapeDtypeStruct((steps * cut, 2 * h), BF16),
        grid_spec=pltpu.PrefetchScalarGridSpec(
            num_scalar_prefetch=1,
            grid=(steps,),
            in_specs=[
                pl.BlockSpec((1, cut, h), lambda i, at: (0, at[i], 0)),
                pl.BlockSpec((1, cut, h), lambda i, at: (0, at[i], 0)),
            ],
            out_specs=pl.BlockSpec((cut, 2 * h), lambda i, at: (i, 0)),
        ),
        compiler_params=pltpu.CompilerParams(vmem_limit_bytes=56 << 20),
        cost_estimate=pl.CostEstimate(
            flops=0, bytes_accessed=8 * steps * cut * h, transcendentals=0
        ),
    )(at, gate, up)


def local(context, out_proj, residual, norm_gain, expert_ids, gates, gate_proj, up_proj, down_proj):
    ny, nc, nz, nx = (lax.axis_size(a) for a in ("y", "c", "z", "x"))
    rows_here, width = residual.shape
    quarter = width // nx
    experts_total = ny * nc * nz
    capacity = min(rows_here, max(2, rows_here * TOPK * 5 // (4 * experts_total)))
    x = lax.axis_index("x")
    c = lax.axis_index("c")
    mate = jnp.where(c == 0, x ^ 1, x ^ 3)
    twin = jnp.where(c == 0, x ^ 3, x ^ 1)
    tokens_core = nx * rows_here
    tokens = nc * tokens_core

    to_mate = lambda value: from_places(value, lambda c, x: (c, mate_of(c, x)))
    to_twin = lambda value: from_places(value, lambda c, x: (c, twin_of(c, x)))

    def cut_down(at):
        return lax.dynamic_slice(
            down_proj[0], (0, at * quarter), (down_proj.shape[1], quarter)
        )

    part = project(context, out_proj, nx)

    meta = jnp.concatenate([expert_ids.astype(BF16), gates], axis=1)
    meta = jnp.pad(meta, ((0, 0), (0, 128 - meta.shape[1])))
    came = [meta] + [shift(meta, "x", k) for k in range(1, nx)]
    part = exchange(part.reshape(nz, tokens_core, width), "z")
    ring = [came[(nx - m) % nx] for m in range(nx)]
    ring = jnp.concatenate(ring + ring[:-1], axis=0)
    meta_own = lax.dynamic_slice(
        ring, (lax.rem(nx - x, nx) * rows_here, jnp.int32(0)), (tokens_core, meta.shape[1])
    )
    meta_all = jnp.concatenate([meta_own, shift(meta_own, "c", 1)], axis=0)
    ids = meta_all[:, :TOPK].astype(jnp.int32)
    gate_vals = meta_all[:, TOPK : 2 * TOPK].astype(F32)

    places = ny * nz
    place = jnp.arange(places, dtype=jnp.int32)
    expert_of = ((place // nz) * nc + c) * nz + lax.rem(place, nz)
    matches = ids[:, :, None] == expert_of[None, None, :]
    picked = jnp.any(matches, axis=1).astype(jnp.int32)
    weighted = jnp.sum(jnp.where(matches, gate_vals[:, :, None], F32(0)), axis=1)
    by_device = picked.reshape(nc * nx, rows_here, places)
    ranking = jnp.cumsum(by_device, axis=1) - by_device
    admitted = (by_device > 0) & (ranking < capacity)
    device_iota = jnp.arange(nc * nx, dtype=jnp.int32)[:, None, None]
    slot = jnp.where(admitted, device_iota * capacity + ranking, -1).reshape(tokens, places)
    slots = nc * nx * capacity
    slot_iota = jnp.arange(slots, dtype=jnp.int32)
    chosen = slot.T[:, None, :] == slot_iota[None, :, None]
    selector = chosen.astype(BF16).reshape(places * slots, tokens)
    scaled = jnp.where(chosen, weighted.T[:, None, :], F32(0)).astype(BF16)
    scaled = scaled.reshape(places * slots, tokens)
    kept = pack(jnp.stack([x, twin]).astype(jnp.int32), gate_proj, up_proj)
    given = bundle(jnp.stack([mate, x ^ 2]).astype(jnp.int32), gate_proj, up_proj, down_proj)
    own_down, twin_cut, far_cut = cut_down(x), cut_down(twin), cut_down(x ^ 2)
    twin_down = to_twin(twin_cut)
    far_down = to_twin(to_mate(far_cut))
    gain = jnp.concatenate(
        [lax.dynamic_slice(norm_gain, (q * quarter,), (quarter,)) for q in (x, twin)]
    )[None, :]
    selector, scaled, part, kept, given, own_down, gain, twin_down, far_down = (
        lax.optimization_barrier(
            (selector, scaled, part, kept, given, own_down, gain, twin_down, far_down)
        )
    )
    parts = owner_sum(x[None].astype(jnp.int32), part, residual, nx)
    came = [parts[0]] + [shift(parts[k], "x", k) for k in (2, 1, 3)]

    hidden = sum(term.astype(F32) for term in came).astype(BF16)
    hidden_wide = hidden.astype(F32)

    twin_own = from_places(hidden, lambda c, x: (c, twin_of(c, x)))
    near_other = from_places(hidden, lambda c, x: (1 - c, x))
    twin_other = from_places(hidden, lambda c, x: (1 - c, twin_of(c, x)))
    twin_own, near_other, twin_other, given = lax.optimization_barrier(
        (twin_own, near_other, twin_other, given)
    )
    rows = jnp.concatenate(
        [
            jnp.concatenate([hidden, near_other], axis=0),
            jnp.concatenate([twin_own, twin_other], axis=0),
        ],
        axis=1,
    )
    outgoing = jnp.dot(selector, rows, preferred_element_type=F32).astype(BF16)
    arrived = exchange(outgoing.reshape(places, slots, 2 * quarter), ("y", "z"))
    arrived = arrived.reshape(places * slots, 2 * quarter)

    taken = to_mate(given)
    arrived, taken = lax.optimization_barrier((arrived, taken))
    gained, square, theirs = first_product(arrived, gain, taken)
    came_back = to_mate(theirs)
    inverse = lax.rsqrt((square + to_mate(square)) / width + 1e-06)
    total = jnp.dot(gained, kept, preferred_element_type=F32)
    total, came_back = lax.optimization_barrier((total, came_back))
    total = total + came_back.astype(F32)
    total = total * inverse
    hid = total.shape[1] // 2
    activated = (jax.nn.silu(total[:, :hid]) * total[:, hid:]).astype(BF16)
    blocks = (activated, to_mate(activated), to_twin(activated), shift(activated, "x", 2))
    result = down_product(blocks, (own_down, taken, twin_down, far_down), 4 * quarter)

    returned = exchange(result.reshape(places, slots, quarter), ("y", "z"))
    returned = returned.reshape(places * slots, quarter)
    mixture = lax.dot_general(
        scaled, returned, (((0,), (0,)), ((), ())), preferred_element_type=F32
    )
    mixture = mixture[:tokens_core] + shift(mixture[tokens_core:], "c", 1)
    out = (hidden_wide + mixture).astype(BF16)
    out = exchange(out.reshape(nx, rows_here, quarter), "x")
    return out.transpose(1, 0, 2).reshape(rows_here, width)


def solution(mesh):
    grid = Mesh(mesh.devices.reshape(4, 2, 4, 4), ("y", "c", "z", "x"))
    group, member = ("y", "c"), ("z", "x")
    owner = group + member
    in_specs = (
        P(group, member),
        P(member, None),
        P(owner, None),
        P(),
        P(owner, None),
        P(owner, None),
        P(owner, None, None),
        P(owner, None, None),
        P(owner, None, None),
    )
    return jax.shard_map(
        local, mesh=grid, in_specs=in_specs, out_specs=P(owner, None), check_vma=False
    )
```

```python
import functools

import jax
import jax.numpy as jnp
from jax import lax
from jax.experimental import pallas as pl
from jax.experimental.pallas import tpu as pltpu
from jax.sharding import Mesh
from jax.sharding import PartitionSpec as P

TOPK = 8
F32 = jnp.float32
BF16 = jnp.bfloat16


def shift(value, axis, amount):
    size = lax.axis_size(axis)
    return lax.ppermute(value, axis, [(i, (i + amount) % size) for i in range(size)])


def exchange(value, axes):
    return lax.all_to_all(value, axes, split_axis=0, concat_axis=0, tiled=True)


def mate_of(c, x):
    return x ^ 1 if c == 0 else x ^ 3


def twin_of(c, x):
    return x ^ 3 if c == 0 else x ^ 1


def from_places(value, source):
    pairs = []
    for c in range(2):
        for x in range(4):
            sc, sx = source(c, x)
            pairs.append((sc * 4 + sx, c * 4 + x))
    return lax.ppermute(value, ("c", "x"), pairs)


def project_body(a_ref, b_ref, o_ref):
    o_ref[...] = jnp.dot(a_ref[...], b_ref[...], preferred_element_type=F32).astype(BF16)


def project(context, weight, blocks):
    rows, depth = context.shape
    width = weight.shape[1]
    step = width // blocks
    return pl.pallas_call(
        project_body,
        out_shape=jax.ShapeDtypeStruct((rows, width), BF16),
        grid=(blocks,),
        in_specs=[
            pl.BlockSpec((rows, depth), lambda q: (0, 0)),
            pl.BlockSpec((depth, step), lambda q: (0, q)),
        ],
        out_specs=pl.BlockSpec((rows, step), lambda q: (0, q)),
        compiler_params=pltpu.CompilerParams(vmem_limit_bytes=56 << 20),
        cost_estimate=pl.CostEstimate(
            flops=2 * rows * depth * width,
            bytes_accessed=2 * (rows * depth + depth * width + rows * width),
            transcendentals=0,
        ),
    )(context, weight)


def owner_sum_body(at_ref, a_ref, r_ref, *refs):
    outs, acc_ref = refs[:-1], refs[-1]
    step = pl.program_id(0)
    own = r_ref.shape[0]
    total = a_ref[0].astype(F32)
    for i in range(1, a_ref.shape[0]):
        total += a_ref[i].astype(F32)
    acc_ref[...] = total
    here = pl.ds(pl.multiple_of(at_ref[0] * own, own), own)
    acc_ref[here, :] += r_ref[...].astype(F32)
    for k, o_ref in enumerate(outs):

        @pl.when(step == k)
        def _():
            o_ref[...] = acc_ref[...].astype(BF16)


def owner_sum(at, terms, residual, blocks):
    count, rows, width = terms.shape
    step = width // blocks
    turn = lambda q, at: lax.rem(at[0] + q, blocks)
    return pl.pallas_call(
        owner_sum_body,
        out_shape=[jax.ShapeDtypeStruct((rows, step), BF16)] * blocks,
        grid_spec=pltpu.PrefetchScalarGridSpec(
            num_scalar_prefetch=1,
            grid=(blocks,),
            in_specs=[
                pl.BlockSpec((count, rows, step), lambda q, at: (0, 0, turn(q, at))),
                pl.BlockSpec((residual.shape[0], step), lambda q, at: (0, turn(q, at))),
            ],
            out_specs=[pl.BlockSpec((rows, step), lambda q, at: (0, 0))] * blocks,
            scratch_shapes=[pltpu.VMEM((rows, step), F32)],
        ),
        compiler_params=pltpu.CompilerParams(vmem_limit_bytes=24 << 20),
        cost_estimate=pl.CostEstimate(
            flops=count * rows * width,
            bytes_accessed=2 * (count + 1) * rows * width,
            transcendentals=0,
        ),
    )(at, terms, residual)


def first_body(a_ref, gain_ref, w_ref, g_ref, s_ref, o_ref):
    depth = a_ref.shape[1]
    h = w_ref.shape[1]
    squares = None
    for at in range(0, depth, 256):
        wide = a_ref[:, at : at + 256].astype(F32)
        for i in range(0, 256, 128):
            part = wide[:, i : i + 128]
            squares = part * part if squares is None else squares + part * part
        g_ref[:, at : at + 256] = (wide * gain_ref[:, at : at + 256]).astype(BF16)
    gained = g_ref[...]
    for i in range(2):
        o_ref[:, i * h : (i + 1) * h] = jnp.dot(
            gained, w_ref[i * depth : (i + 1) * depth, :], preferred_element_type=F32
        ).astype(BF16)
    s_ref[...] = jnp.sum(squares, axis=1, keepdims=True)


WHOLE = pl.BlockSpec(memory_space=pltpu.VMEM)


def first_product(arrived, gain, weight):
    rows, depth = arrived.shape
    cols = 2 * weight.shape[1]
    return pl.pallas_call(
        first_body,
        out_shape=(
            jax.ShapeDtypeStruct((rows, depth), BF16),
            jax.ShapeDtypeStruct((rows, 1), F32),
            jax.ShapeDtypeStruct((rows, cols), BF16),
        ),
        in_specs=[WHOLE] * 3,
        out_specs=(WHOLE,) * 3,
        compiler_params=pltpu.CompilerParams(vmem_limit_bytes=32 << 20),
        cost_estimate=pl.CostEstimate(
            flops=2 * rows * depth * cols,
            bytes_accessed=2 * (2 * rows * depth + depth * cols + rows * cols),
            transcendentals=0,
        ),
    )(arrived, gain, weight)


def down_body(start, *refs):
    own, from_mate, from_twin, from_far, w_own, w_mate, w_twin, w_far, o_ref = refs
    h = own.shape[1]
    for j in range(o_ref.shape[1] // h):
        cols = slice(j * h, (j + 1) * h)
        at = slice(start + j * h, start + (j + 1) * h)
        total = jnp.dot(own[...], w_own[:, cols], preferred_element_type=F32)
        total += jnp.dot(from_mate[...], w_mate[at, :], preferred_element_type=F32)
        total += jnp.dot(from_twin[...], w_twin[:, cols], preferred_element_type=F32)
        total += jnp.dot(from_far[...], w_far[:, cols], preferred_element_type=F32)
        o_ref[:, cols] = total.astype(BF16)


def down_product(blocks, weights, start):
    rows, h = blocks[0].shape
    cols = weights[0].shape[1]
    return pl.pallas_call(
        functools.partial(down_body, start),
        out_shape=jax.ShapeDtypeStruct((rows, cols), BF16),
        in_specs=[WHOLE] * 8,
        out_specs=WHOLE,
        compiler_params=pltpu.CompilerParams(vmem_limit_bytes=32 << 20),
        cost_estimate=pl.CostEstimate(
            flops=8 * rows * h * cols,
            bytes_accessed=2 * (4 * rows * h + 4 * h * cols + rows * cols),
            transcendentals=0,
        ),
    )(*blocks, *weights)


def bundle_body(at_ref, g_ref, u_ref, d_ref, o_ref):
    step = pl.program_id(0)
    h = o_ref.shape[1]

    @pl.when(step < 2)
    def _():
        o_ref[...] = g_ref[0]

    @pl.when((step >= 2) & (step < 4))
    def _():
        o_ref[...] = u_ref[0]

    @pl.when(step >= 4)
    def _():
        for j in range(d_ref.shape[2] // h):
            o_ref[j * h : (j + 1) * h, :] = d_ref[0, :, j * h : (j + 1) * h]


def bundle(at, gate, up, down):
    deep, h = gate.shape[1:]
    cut = deep // 4

    gate_at = lambda i, at: at[jnp.where(i <= 0, 0, 1)]
    up_at = lambda i, at: at[jnp.where(i <= 2, 0, 1)]
    return pl.pallas_call(
        bundle_body,
        out_shape=jax.ShapeDtypeStruct((5 * cut, h), BF16),
        grid_spec=pltpu.PrefetchScalarGridSpec(
            num_scalar_prefetch=1,
            grid=(5,),
            in_specs=[
                pl.BlockSpec((1, cut, h), lambda i, at: (0, gate_at(i, at), 0)),
                pl.BlockSpec((1, cut, h), lambda i, at: (0, up_at(i, at), 0)),
                pl.BlockSpec((1, h, cut), lambda i, at: (0, 0, at[0])),
            ],
            out_specs=pl.BlockSpec((cut, h), lambda i, at: (i, 0)),
        ),
        compiler_params=pltpu.CompilerParams(vmem_limit_bytes=56 << 20),
        cost_estimate=pl.CostEstimate(
            flops=0, bytes_accessed=20 * cut * h, transcendentals=0
        ),
    )(at, gate, up, down)


def pack_body(at_ref, g_ref, u_ref, o_ref):
    h = g_ref.shape[2]
    o_ref[:, :h] = g_ref[0]
    o_ref[:, h:] = u_ref[0]


def pack(at, gate, up):
    deep, h = gate.shape[1:]
    cut = deep // 4
    steps = at.shape[0]
    return pl.pallas_call(
        pack_body,
        out_shape=jax.ShapeDtypeStruct((steps * cut, 2 * h), BF16),
        grid_spec=pltpu.PrefetchScalarGridSpec(
            num_scalar_prefetch=1,
            grid=(steps,),
            in_specs=[
                pl.BlockSpec((1, cut, h), lambda i, at: (0, at[i], 0)),
                pl.BlockSpec((1, cut, h), lambda i, at: (0, at[i], 0)),
            ],
            out_specs=pl.BlockSpec((cut, 2 * h), lambda i, at: (i, 0)),
        ),
        compiler_params=pltpu.CompilerParams(vmem_limit_bytes=56 << 20),
        cost_estimate=pl.CostEstimate(
            flops=0, bytes_accessed=8 * steps * cut * h, transcendentals=0
        ),
    )(at, gate, up)


def local(context, out_proj, residual, norm_gain, expert_ids, gates, gate_proj, up_proj, down_proj):
    ny, nc, nz, nx = (lax.axis_size(a) for a in ("y", "c", "z", "x"))
    rows_here, width = residual.shape
    quarter = width // nx
    experts_total = ny * nc * nz
    capacity = min(rows_here, max(2, rows_here * TOPK * 5 // (4 * experts_total)))
    x = lax.axis_index("x")
    c = lax.axis_index("c")
    mate = jnp.where(c == 0, x ^ 1, x ^ 3)
    twin = jnp.where(c == 0, x ^ 3, x ^ 1)
    tokens_core = nx * rows_here
    tokens = nc * tokens_core

    to_mate = lambda value: from_places(value, lambda c, x: (c, mate_of(c, x)))
    to_twin = lambda value: from_places(value, lambda c, x: (c, twin_of(c, x)))

    def cut_down(at):
        return lax.dynamic_slice(
            down_proj[0], (0, at * quarter), (down_proj.shape[1], quarter)
        )

    part = project(context, out_proj, nx // 2)

    meta = jnp.concatenate([expert_ids.astype(BF16), gates], axis=1)
    meta = jnp.pad(meta, ((0, 0), (0, 128 - meta.shape[1])))
    came = [meta] + [shift(meta, "x", k) for k in range(1, nx)]
    part = exchange(part.reshape(nz, tokens_core, width), "z")
    ring = [came[(nx - m) % nx] for m in range(nx)]
    ring = jnp.concatenate(ring + ring[:-1], axis=0)
    meta_own = lax.dynamic_slice(
        ring, (lax.rem(nx - x, nx) * rows_here, jnp.int32(0)), (tokens_core, meta.shape[1])
    )
    meta_all = jnp.concatenate([meta_own, shift(meta_own, "c", 1)], axis=0)
    ids = meta_all[:, :TOPK].astype(jnp.int32)
    gate_vals = meta_all[:, TOPK : 2 * TOPK].astype(F32)

    places = ny * nz
    place = jnp.arange(places, dtype=jnp.int32)
    expert_of = ((place // nz) * nc + c) * nz + lax.rem(place, nz)
    matches = ids[:, :, None] == expert_of[None, None, :]
    picked = jnp.any(matches, axis=1).astype(jnp.int32)
    weighted = jnp.sum(jnp.where(matches, gate_vals[:, :, None], F32(0)), axis=1)
    by_device = picked.reshape(nc * nx, rows_here, places)
    ranking = jnp.cumsum(by_device, axis=1) - by_device
    admitted = (by_device > 0) & (ranking < capacity)
    device_iota = jnp.arange(nc * nx, dtype=jnp.int32)[:, None, None]
    slot = jnp.where(admitted, device_iota * capacity + ranking, -1).reshape(tokens, places)
    slots = nc * nx * capacity
    slot_iota = jnp.arange(slots, dtype=jnp.int32)
    chosen = slot.T[:, None, :] == slot_iota[None, :, None]
    selector = chosen.astype(BF16).reshape(places * slots, tokens)
    scaled = jnp.where(chosen, weighted.T[:, None, :], F32(0)).astype(BF16)
    scaled = scaled.reshape(places * slots, tokens)
    kept = pack(jnp.stack([x, twin]).astype(jnp.int32), gate_proj, up_proj)
    given = bundle(jnp.stack([mate, x ^ 2]).astype(jnp.int32), gate_proj, up_proj, down_proj)
    own_down, twin_cut, far_cut = cut_down(x), cut_down(twin), cut_down(x ^ 2)
    twin_down = to_twin(twin_cut)
    far_down = to_twin(to_mate(far_cut))
    gain = jnp.concatenate(
        [lax.dynamic_slice(norm_gain, (q * quarter,), (quarter,)) for q in (x, twin)]
    )[None, :]
    selector, scaled, part, kept, given, own_down, gain, twin_down, far_down = (
        lax.optimization_barrier(
            (selector, scaled, part, kept, given, own_down, gain, twin_down, far_down)
        )
    )
    parts = owner_sum(x[None].astype(jnp.int32), part, residual, nx)
    came = [parts[0]] + [shift(parts[k], "x", k) for k in (2, 1, 3)]

    hidden = sum(term.astype(F32) for term in came).astype(BF16)
    hidden_wide = hidden.astype(F32)

    twin_own = from_places(hidden, lambda c, x: (c, twin_of(c, x)))
    near_other = from_places(hidden, lambda c, x: (1 - c, x))
    twin_other = from_places(hidden, lambda c, x: (1 - c, twin_of(c, x)))
    twin_own, near_other, twin_other, given = lax.optimization_barrier(
        (twin_own, near_other, twin_other, given)
    )
    rows = jnp.concatenate(
        [
            jnp.concatenate([hidden, near_other], axis=0),
            jnp.concatenate([twin_own, twin_other], axis=0),
        ],
        axis=1,
    )
    outgoing = jnp.dot(selector, rows, preferred_element_type=F32).astype(BF16)
    arrived = exchange(outgoing.reshape(places, slots, 2 * quarter), ("y", "z"))
    arrived = arrived.reshape(places * slots, 2 * quarter)

    taken = to_mate(given)
    arrived, taken = lax.optimization_barrier((arrived, taken))
    gained, square, theirs = first_product(arrived, gain, taken)
    came_back = to_mate(theirs)
    inverse = lax.rsqrt((square + to_mate(square)) / width + 1e-06)
    total = jnp.dot(gained, kept, preferred_element_type=F32)
    total, came_back = lax.optimization_barrier((total, came_back))
    total = total + came_back.astype(F32)
    total = total * inverse
    hid = total.shape[1] // 2
    activated = (jax.nn.silu(total[:, :hid]) * total[:, hid:]).astype(BF16)
    blocks = (activated, to_mate(activated), to_twin(activated), shift(activated, "x", 2))
    result = down_product(blocks, (own_down, taken, twin_down, far_down), 4 * quarter)

    returned = exchange(result.reshape(places, slots, quarter), ("y", "z"))
    returned = returned.reshape(places * slots, quarter)
    mixture = lax.dot_general(
        scaled, returned, (((0,), (0,)), ((), ())), preferred_element_type=F32
    )
    mixture = mixture[:tokens_core] + shift(mixture[tokens_core:], "c", 1)
    out = (hidden_wide + mixture).astype(BF16)
    out = exchange(out.reshape(nx, rows_here, quarter), "x")
    return out.transpose(1, 0, 2).reshape(rows_here, width)


def solution(mesh):
    grid = Mesh(mesh.devices.reshape(4, 2, 4, 4), ("y", "c", "z", "x"))
    group, member = ("y", "c"), ("z", "x")
    owner = group + member
    in_specs = (
        P(group, member),
        P(member, None),
        P(owner, None),
        P(),
        P(owner, None),
        P(owner, None),
        P(owner, None, None),
        P(owner, None, None),
        P(owner, None, None),
    )
    return jax.shard_map(
        local, mesh=grid, in_specs=in_specs, out_specs=P(owner, None), check_vma=False
    )
```

```python
import functools

import jax
import jax.numpy as jnp
from jax import lax
from jax.experimental import pallas as pl
from jax.experimental.pallas import tpu as pltpu
from jax.sharding import Mesh
from jax.sharding import PartitionSpec as P

TOPK = 8
F32 = jnp.float32
BF16 = jnp.bfloat16


def shift(value, axis, amount):
    size = lax.axis_size(axis)
    return lax.ppermute(value, axis, [(i, (i + amount) % size) for i in range(size)])


def exchange(value, axes):
    return lax.all_to_all(value, axes, split_axis=0, concat_axis=0, tiled=True)


def mate_of(c, x):
    return x ^ 1 if c == 0 else x ^ 3


def twin_of(c, x):
    return x ^ 3 if c == 0 else x ^ 1


def from_places(value, source):
    pairs = []
    for c in range(2):
        for x in range(4):
            sc, sx = source(c, x)
            pairs.append((sc * 4 + sx, c * 4 + x))
    return lax.ppermute(value, ("c", "x"), pairs)


def project_body(a_ref, b_ref, o_ref):
    o_ref[...] = jnp.dot(a_ref[...], b_ref[...], preferred_element_type=F32).astype(BF16)


def project(context, weight, blocks):
    rows, depth = context.shape
    width = weight.shape[1]
    step = width // blocks
    return pl.pallas_call(
        project_body,
        out_shape=jax.ShapeDtypeStruct((rows, width), BF16),
        grid=(blocks,),
        in_specs=[
            pl.BlockSpec((rows, depth), lambda q: (0, 0)),
            pl.BlockSpec((depth, step), lambda q: (0, q)),
        ],
        out_specs=pl.BlockSpec((rows, step), lambda q: (0, q)),
        compiler_params=pltpu.CompilerParams(vmem_limit_bytes=56 << 20),
        cost_estimate=pl.CostEstimate(
            flops=2 * rows * depth * width,
            bytes_accessed=2 * (rows * depth + depth * width + rows * width),
            transcendentals=0,
        ),
    )(context, weight)


def owner_sum_body(at_ref, a_ref, r_ref, *refs):
    outs, acc_ref = refs[:-1], refs[-1]
    step = pl.program_id(0)
    own = r_ref.shape[0]
    total = a_ref[0].astype(F32)
    for i in range(1, a_ref.shape[0]):
        total += a_ref[i].astype(F32)
    acc_ref[...] = total
    here = pl.ds(pl.multiple_of(at_ref[0] * own, own), own)
    acc_ref[here, :] += r_ref[...].astype(F32)
    for k, o_ref in enumerate(outs):

        @pl.when(step == k)
        def _():
            o_ref[...] = acc_ref[...].astype(BF16)


def owner_sum(at, terms, residual, blocks):
    count, rows, width = terms.shape
    step = width // blocks
    turn = lambda q, at: lax.rem(at[0] + q, blocks)
    return pl.pallas_call(
        owner_sum_body,
        out_shape=[jax.ShapeDtypeStruct((rows, step), BF16)] * blocks,
        grid_spec=pltpu.PrefetchScalarGridSpec(
            num_scalar_prefetch=1,
            grid=(blocks,),
            in_specs=[
                pl.BlockSpec((count, rows, step), lambda q, at: (0, 0, turn(q, at))),
                pl.BlockSpec((residual.shape[0], step), lambda q, at: (0, turn(q, at))),
            ],
            out_specs=[pl.BlockSpec((rows, step), lambda q, at: (0, 0))] * blocks,
            scratch_shapes=[pltpu.VMEM((rows, step), F32)],
        ),
        compiler_params=pltpu.CompilerParams(vmem_limit_bytes=24 << 20),
        cost_estimate=pl.CostEstimate(
            flops=count * rows * width,
            bytes_accessed=2 * (count + 1) * rows * width,
            transcendentals=0,
        ),
    )(at, terms, residual)


def first_body(a_ref, gain_ref, w_ref, g_ref, s_ref, o_ref):
    depth = a_ref.shape[1]
    h = w_ref.shape[1]
    squares = None
    for at in range(0, depth, 256):
        wide = a_ref[:, at : at + 256].astype(F32)
        for i in range(0, 256, 128):
            part = wide[:, i : i + 128]
            squares = part * part if squares is None else squares + part * part
        g_ref[:, at : at + 256] = (wide * gain_ref[:, at : at + 256]).astype(BF16)
    gained = g_ref[...]
    for i in range(2):
        o_ref[:, i * h : (i + 1) * h] = jnp.dot(
            gained, w_ref[i * depth : (i + 1) * depth, :], preferred_element_type=F32
        ).astype(BF16)
    s_ref[...] = jnp.sum(squares, axis=1, keepdims=True)


WHOLE = pl.BlockSpec(memory_space=pltpu.VMEM)


def first_product(arrived, gain, weight):
    rows, depth = arrived.shape
    cols = 2 * weight.shape[1]
    return pl.pallas_call(
        first_body,
        out_shape=(
            jax.ShapeDtypeStruct((rows, depth), BF16),
            jax.ShapeDtypeStruct((rows, 1), F32),
            jax.ShapeDtypeStruct((rows, cols), BF16),
        ),
        in_specs=[WHOLE] * 3,
        out_specs=(WHOLE,) * 3,
        compiler_params=pltpu.CompilerParams(vmem_limit_bytes=32 << 20),
        cost_estimate=pl.CostEstimate(
            flops=2 * rows * depth * cols,
            bytes_accessed=2 * (2 * rows * depth + depth * cols + rows * cols),
            transcendentals=0,
        ),
    )(arrived, gain, weight)


def down_body(start, *refs):
    own, from_mate, from_twin, from_far, w_own, w_mate, w_twin, w_far, o_ref = refs
    h = own.shape[1]
    for j in range(o_ref.shape[1] // h):
        cols = slice(j * h, (j + 1) * h)
        at = slice(start + j * h, start + (j + 1) * h)
        total = jnp.dot(own[...], w_own[:, cols], preferred_element_type=F32)
        total += jnp.dot(from_mate[...], w_mate[at, :], preferred_element_type=F32)
        total += jnp.dot(from_twin[...], w_twin[:, cols], preferred_element_type=F32)
        total += jnp.dot(from_far[...], w_far[:, cols], preferred_element_type=F32)
        o_ref[:, cols] = total.astype(BF16)


def down_product(blocks, weights, start):
    rows, h = blocks[0].shape
    cols = weights[0].shape[1]
    return pl.pallas_call(
        functools.partial(down_body, start),
        out_shape=jax.ShapeDtypeStruct((rows, cols), BF16),
        in_specs=[WHOLE] * 8,
        out_specs=WHOLE,
        compiler_params=pltpu.CompilerParams(vmem_limit_bytes=32 << 20),
        cost_estimate=pl.CostEstimate(
            flops=8 * rows * h * cols,
            bytes_accessed=2 * (4 * rows * h + 4 * h * cols + rows * cols),
            transcendentals=0,
        ),
    )(*blocks, *weights)


def bundle_body(at_ref, g_ref, u_ref, d_ref, o_ref):
    step = pl.program_id(0)
    h = o_ref.shape[1]

    @pl.when(step < 2)
    def _():
        o_ref[...] = g_ref[0]

    @pl.when((step >= 2) & (step < 4))
    def _():
        o_ref[...] = u_ref[0]

    @pl.when(step >= 4)
    def _():
        for j in range(d_ref.shape[2] // h):
            o_ref[j * h : (j + 1) * h, :] = d_ref[0, :, j * h : (j + 1) * h]


def bundle(at, gate, up, down):
    deep, h = gate.shape[1:]
    cut = deep // 4

    gate_at = lambda i, at: at[jnp.where(i <= 0, 0, 1)]
    up_at = lambda i, at: at[jnp.where(i <= 2, 0, 1)]
    return pl.pallas_call(
        bundle_body,
        out_shape=jax.ShapeDtypeStruct((5 * cut, h), BF16),
        grid_spec=pltpu.PrefetchScalarGridSpec(
            num_scalar_prefetch=1,
            grid=(5,),
            in_specs=[
                pl.BlockSpec((1, cut, h), lambda i, at: (0, gate_at(i, at), 0)),
                pl.BlockSpec((1, cut, h), lambda i, at: (0, up_at(i, at), 0)),
                pl.BlockSpec((1, h, cut), lambda i, at: (0, 0, at[0])),
            ],
            out_specs=pl.BlockSpec((cut, h), lambda i, at: (i, 0)),
        ),
        compiler_params=pltpu.CompilerParams(vmem_limit_bytes=56 << 20),
        cost_estimate=pl.CostEstimate(
            flops=0, bytes_accessed=20 * cut * h, transcendentals=0
        ),
    )(at, gate, up, down)


def pack_body(at_ref, g_ref, u_ref, o_ref):
    h = g_ref.shape[2]
    o_ref[:, :h] = g_ref[0]
    o_ref[:, h:] = u_ref[0]


def pack(at, gate, up):
    deep, h = gate.shape[1:]
    cut = deep // 4
    steps = at.shape[0]
    return pl.pallas_call(
        pack_body,
        out_shape=jax.ShapeDtypeStruct((steps * cut, 2 * h), BF16),
        grid_spec=pltpu.PrefetchScalarGridSpec(
            num_scalar_prefetch=1,
            grid=(steps,),
            in_specs=[
                pl.BlockSpec((1, cut, h), lambda i, at: (0, at[i], 0)),
                pl.BlockSpec((1, cut, h), lambda i, at: (0, at[i], 0)),
            ],
            out_specs=pl.BlockSpec((cut, 2 * h), lambda i, at: (i, 0)),
        ),
        compiler_params=pltpu.CompilerParams(vmem_limit_bytes=56 << 20),
        cost_estimate=pl.CostEstimate(
            flops=0, bytes_accessed=8 * steps * cut * h, transcendentals=0
        ),
    )(at, gate, up)


def local(context, out_proj, residual, norm_gain, expert_ids, gates, gate_proj, up_proj, down_proj):
    ny, nc, nz, nx = (lax.axis_size(a) for a in ("y", "c", "z", "x"))
    rows_here, width = residual.shape
    quarter = width // nx
    experts_total = ny * nc * nz
    capacity = min(rows_here, max(2, rows_here * TOPK * 5 // (4 * experts_total)))
    x = lax.axis_index("x")
    c = lax.axis_index("c")
    mate = jnp.where(c == 0, x ^ 1, x ^ 3)
    twin = jnp.where(c == 0, x ^ 3, x ^ 1)
    tokens_core = nx * rows_here
    tokens = nc * tokens_core

    to_mate = lambda value: from_places(value, lambda c, x: (c, mate_of(c, x)))
    to_twin = lambda value: from_places(value, lambda c, x: (c, twin_of(c, x)))

    def cut_down(at):
        return lax.dynamic_slice(
            down_proj[0], (0, at * quarter), (down_proj.shape[1], quarter)
        )

    part = project(context, out_proj, nx // 2)

    meta = jnp.concatenate([expert_ids.astype(BF16), gates], axis=1)
    meta = jnp.pad(meta, ((0, 0), (0, 128 - meta.shape[1])))
    came = [meta] + [shift(meta, "x", k) for k in range(1, nx)]
    part = exchange(part.reshape(nz, tokens_core, width), "z")
    ring = [came[(nx - m) % nx] for m in range(nx)]
    ring = jnp.concatenate(ring + ring[:-1], axis=0)
    meta_own = lax.dynamic_slice(
        ring, (lax.rem(nx - x, nx) * rows_here, jnp.int32(0)), (tokens_core, meta.shape[1])
    )
    meta_all = jnp.concatenate([meta_own, shift(meta_own, "c", 1)], axis=0)
    ids = meta_all[:, :TOPK].astype(jnp.int32)
    gate_vals = meta_all[:, TOPK : 2 * TOPK].astype(F32)

    places = ny * nz
    place = jnp.arange(places, dtype=jnp.int32)
    expert_of = ((place // nz) * nc + c) * nz + lax.rem(place, nz)
    matches = ids[:, :, None] == expert_of[None, None, :]
    picked = jnp.any(matches, axis=1).astype(jnp.int32)
    weighted = jnp.sum(jnp.where(matches, gate_vals[:, :, None], F32(0)), axis=1)
    by_device = picked.reshape(nc * nx, rows_here, places)
    ranking = jnp.cumsum(by_device, axis=1) - by_device
    admitted = (by_device > 0) & (ranking < capacity)
    device_iota = jnp.arange(nc * nx, dtype=jnp.int32)[:, None, None]
    slot = jnp.where(admitted, device_iota * capacity + ranking, -1).reshape(tokens, places)
    slots = nc * nx * capacity
    slot_iota = jnp.arange(slots, dtype=jnp.int32)
    chosen = slot.T[:, None, :] == slot_iota[None, :, None]
    selector = chosen.astype(BF16).reshape(places * slots, tokens)
    scaled = jnp.where(chosen, weighted.T[:, None, :], F32(0)).astype(BF16)
    scaled = scaled.reshape(places * slots, tokens)
    kept = pack(jnp.stack([x, twin]).astype(jnp.int32), gate_proj, up_proj)
    given = bundle(jnp.stack([mate, x ^ 2]).astype(jnp.int32), gate_proj, up_proj, down_proj)
    own_down, twin_cut, far_cut = cut_down(x), cut_down(twin), cut_down(x ^ 2)
    twin_down = to_twin(twin_cut)
    far_down = to_twin(to_mate(far_cut))
    gain = jnp.concatenate(
        [lax.dynamic_slice(norm_gain, (q * quarter,), (quarter,)) for q in (x, twin)]
    )[None, :]
    selector, scaled, part, kept, given, own_down, gain, twin_down, far_down = (
        lax.optimization_barrier(
            (selector, scaled, part, kept, given, own_down, gain, twin_down, far_down)
        )
    )
    parts = owner_sum(x[None].astype(jnp.int32), part, residual, nx)
    came = [parts[0]] + [shift(parts[k], "x", k) for k in (2, 1, 3)]

    hidden = sum(term.astype(F32) for term in came).astype(BF16)
    hidden_wide = hidden.astype(F32)

    twin_own = from_places(hidden, lambda c, x: (c, twin_of(c, x)))
    near_other = from_places(hidden, lambda c, x: (1 - c, x))
    twin_other = from_places(hidden, lambda c, x: (1 - c, twin_of(c, x)))
    twin_own, near_other, twin_other, given = lax.optimization_barrier(
        (twin_own, near_other, twin_other, given)
    )
    rows = jnp.concatenate(
        [
            jnp.concatenate([hidden, near_other], axis=0),
            jnp.concatenate([twin_own, twin_other], axis=0),
        ],
        axis=1,
    )
    outgoing = jnp.dot(selector, rows, preferred_element_type=F32).astype(BF16)
    arrived = exchange(outgoing.reshape(places, slots, 2 * quarter), ("y", "z"))
    arrived = arrived.reshape(places * slots, 2 * quarter)

    taken = to_mate(given)
    arrived, taken = lax.optimization_barrier((arrived, taken))
    gained, square, theirs = first_product(arrived, gain, taken)
    came_back = to_mate(theirs)
    inverse = lax.rsqrt((square + to_mate(square)) / width + 1e-06)
    total = jnp.dot(gained, kept, preferred_element_type=F32)
    total, came_back = lax.optimization_barrier((total, came_back))
    total = total + came_back.astype(F32)
    total = total * inverse
    hid = total.shape[1] // 2
    activated = (jax.nn.silu(total[:, :hid]) * total[:, hid:]).astype(BF16)
    blocks = (activated, to_mate(activated), to_twin(activated), shift(activated, "x", 2))
    result = down_product(blocks, (own_down, taken, twin_down, far_down), 4 * quarter)

    returned = exchange(result.reshape(places, slots, quarter), ("y", "z"))
    returned = returned.reshape(places * slots, quarter)
    mixture = lax.dot_general(
        scaled, returned, (((0,), (0,)), ((), ())), preferred_element_type=F32
    )
    mixture = mixture[:tokens_core] + shift(mixture[tokens_core:], "c", 1)
    out = (hidden_wide + mixture).astype(BF16)
    came = []
    for k in range(nx):
        at = lax.rem(x + k, nx) * rows_here
        piece = lax.dynamic_slice(out, (at, jnp.int32(0)), (rows_here, quarter))
        came.append(piece if k == 0 else shift(piece, "x", k))
    ring = [came[(nx - m) % nx] for m in range(nx)]
    ring = jnp.concatenate(ring + ring[:-1], axis=1)
    return lax.dynamic_slice(ring, (jnp.int32(0), lax.rem(nx - x, nx) * quarter), (rows_here, width))


def solution(mesh):
    grid = Mesh(mesh.devices.reshape(4, 2, 4, 4), ("y", "c", "z", "x"))
    group, member = ("y", "c"), ("z", "x")
    owner = group + member
    in_specs = (
        P(group, member),
        P(member, None),
        P(owner, None),
        P(),
        P(owner, None),
        P(owner, None),
        P(owner, None, None),
        P(owner, None, None),
        P(owner, None, None),
    )
    return jax.shard_map(
        local, mesh=grid, in_specs=in_specs, out_specs=P(owner, None), check_vma=False
    )
```
